128 devices in a mesh: leaf: 128 (over y, z, x, core).
Axes of the slice: x: 4, y: 4, z: 4, core: 2. Of those that a mesh axis runs over, the one named last changes fastest.
Arguments:
- points: float32 [16, 262144], P(None, 'leaf'), may hold values from -6 to 6
- charges: float32 [16, 262144], P(None, 'leaf'), may hold values from -0.6 to 0.6
- near_list: int32 [512, 32], P('leaf'), may hold values from 0 to 511, as said below
- near_count: int32 [512], P('leaf'), may hold values from 1 to 32, as said below
- leaf_basis: float32 [262144, 256], P('leaf'), may hold values from -0.75 to 0.75
- device_basis: float32 [131072, 256], P('leaf'), may hold values from -0.1875 to 0.1875
- device_skeleton: int32 [128, 256], P('leaf'), may hold values from 0 to 2047, as said below
- group_basis: float32 [1024, 8192], P(None, 'leaf'), may hold values from -0.1875 to 0.1875
- group_skeleton: int32 [8192], P('leaf'), may hold values from 0 to 1023, as said below
- cluster_basis: float32 [1024, 2048], P(None, 'leaf'), may hold values from -0.1875 to 0.1875
- cluster_skeleton: int32 [2048], P('leaf'), may hold values from 0 to 1023, as said below
Outputs:
- potentials: float32 [16, 262144], P(None, 'leaf')
The draws below stay inside these ranges and needn't reach their ends.
Inputs may be any that keep to these rules, and one draw needn't show every extreme that they name: `near_list`: row l names leaves whose devices lie at most 8 devices from leaf l's device; its first entry is l, its first near_count[l] entries are distinct, and the later entries repeat l. Only the first near_count[l] entries of leaf l's list count. `device_skeleton`: each row holds distinct indices into its device's points. `group_skeleton`: entries g * 256 to (g + 1) * 256 - 1 are distinct indices into the 1024 skeleton points of group g's four devices, side by side in device order. `cluster_skeleton`: entries c * 256 to (c + 1) * 256 - 1 are distinct indices into the 1024 skeleton points of cluster c's four groups, side by side in group order.
All inputs are finite; a program needn't handle non-finite values.
Results may differ from the reference program's by a relative error of at most 0.0034.
Values sent between devices are 32-bit elements; how exact they have to be, the bound alone decides.
No kernel may reach another device: no remote copies, remote signals or barrier semaphores. Data moves between devices by JAX's collectives and lax.ppermute only.
A program may use at most 64 MiB of HBM per device.

```python
import jax
import jax.numpy as jnp
from jax import lax

F = 16
R = 16
LEAF = 512
S = 256
NBR = 32
REACH = 8
LEAVES_DEV = 4
NLEAVES = 512
NPTS = 262144
N_LEAF = 128


def near_tables(key):
    base_key = jax.random.fold_in(key, 17)
    device_total = NLEAVES // LEAVES_DEV
    span = (2 * REACH + 1) * LEAVES_DEV
    leaves = jnp.arange(NLEAVES, dtype=jnp.int32)
    owners = leaves // LEAVES_DEV
    offsets = jnp.arange(span, dtype=jnp.int32)
    candidates = (owners[:, None] - REACH) * LEAVES_DEV + offsets[None, :]
    usable = (candidates >= 0) & (candidates < NLEAVES) & (candidates != leaves[:, None])
    noise = jax.random.randint(jax.random.fold_in(base_key, 1), (NLEAVES, span), 0, 1 << 18)
    scores = jnp.where(usable, noise * 1024 + offsets[None, :], (1 << 29) + offsets[None, :])
    order = jnp.argsort(scores, axis=1)
    chosen = jnp.take_along_axis(candidates, order[:, :NBR - 1], axis=1)
    usable_count = jnp.sum(usable.astype(jnp.int32), axis=1)
    device_load = jax.random.randint(jax.random.fold_in(base_key, 2), (device_total,), 1, 5)
    drawn = jax.random.randint(jax.random.fold_in(base_key, 3), (NLEAVES,), 0, 1 << 20)
    ceiling = 8 * device_load[owners]
    counts = 1 + drawn % ceiling
    fullest = jax.random.randint(jax.random.fold_in(base_key, 4), (), REACH * LEAVES_DEV, NLEAVES - REACH * LEAVES_DEV)
    emptiest = jax.random.randint(jax.random.fold_in(base_key, 5), (), 0, REACH * LEAVES_DEV)
    counts = jnp.where(leaves == fullest, NBR, counts)
    counts = jnp.where(leaves == emptiest, 1, counts)
    counts = jnp.minimum(counts, 1 + usable_count)
    lists = jnp.concatenate([leaves[:, None], chosen], axis=1)
    slots = jnp.arange(NBR, dtype=jnp.int32)
    lists = jnp.where(slots[None, :] < counts[:, None], lists, leaves[:, None])
    return (lists.astype(jnp.int32), counts.astype(jnp.int32))


def draw_near_list(key, part):
    return near_tables(key)[0]


def draw_near_count(key, part):
    return near_tables(key)[1]


def node_skeleton(key, nodes, pool, picks):
    node_keys = jax.random.split(key, nodes)
    orders = jax.vmap(lambda one_key: jax.random.permutation(one_key, pool))(node_keys)
    marked = jax.random.randint(jax.random.fold_in(key, 7), (), 0, nodes)
    chosen_row = orders[marked]
    spot_high = jnp.argmax(chosen_row == pool - 1)
    chosen_row = chosen_row.at[spot_high].set(chosen_row[0]).at[0].set(pool - 1)
    spot_low = jnp.argmax(chosen_row == 0)
    chosen_row = chosen_row.at[spot_low].set(chosen_row[1]).at[1].set(0)
    orders = orders.at[marked].set(chosen_row)
    return orders[:, :picks].astype(jnp.int32)


def draw_device_skeleton(key, part):
    return node_skeleton(jax.random.fold_in(key, 31), NLEAVES // LEAVES_DEV, LEAVES_DEV * LEAF, S)


def draw_group_skeleton(key, part):
    return node_skeleton(jax.random.fold_in(key, 37), NLEAVES // LEAVES_DEV // 4, 4 * S, S).reshape(-1)


def draw_cluster_skeleton(key, part):
    return node_skeleton(jax.random.fold_in(key, 41), NLEAVES // LEAVES_DEV // 16, 4 * S, S).reshape(-1)


def block_levels(key, dims, pieces, low, top_value):
    gain, own = 1.0, jax.random.fold_in(key, 6)
    for position, parts in pieces:
        steps = jnp.exp(jax.random.uniform(jax.random.fold_in(own, position), (parts,), jnp.float32, low / len(pieces), top_value / len(pieces)))
        gain = gain * jnp.repeat(steps, dims[position] // parts).reshape([-1 if axis == position else 1 for axis in range(len(dims))])
    return gain


def centred(rng, dims, width, most, cuts=(), kind=jnp.bfloat16):
    loudness = block_levels(rng, dims, cuts, -0.22, 0.18) if cuts else 1.0
    values = jax.random.normal(rng, dims, jnp.float32) * width * loudness
    return jnp.minimum(jnp.maximum(values, -most), most).astype(kind)


def setup_inputs(seed: int = 0) -> dict:
    streams_of = jax.random.split(jax.random.key(seed), 12)
    points = centred(streams_of[0], (F, NPTS), 1.0, 6.0, ((1, 128),), jnp.float32)
    charges = centred(streams_of[1], (R, NPTS), 0.1, 0.6, ((1, 128),), jnp.float32)
    near_list = draw_near_list(jax.random.fold_in(streams_of[11], 71), 0)
    near_count = draw_near_count(jax.random.fold_in(streams_of[11], 71), 0)
    leaf_basis = centred(streams_of[4], (NPTS, S), (S // 4) ** -0.5, 0.75, ((0, 128),), jnp.float32)
    device_basis = centred(streams_of[5], (NLEAVES * S, S), (LEAVES_DEV * S) ** -0.5, 0.1875, ((0, 128),), jnp.float32)
    device_skeleton = draw_device_skeleton(jax.random.fold_in(streams_of[11], 71), 0)
    group_basis = centred(streams_of[7], (4 * S, N_LEAF * S // 4), (4 * S) ** -0.5, 0.1875, ((1, 128),), jnp.float32)
    group_skeleton = draw_group_skeleton(jax.random.fold_in(streams_of[11], 71), 0)
    cluster_basis = centred(streams_of[9], (4 * S, N_LEAF * S // 16), (4 * S) ** -0.5, 0.1875, ((1, 128),), jnp.float32)
    cluster_skeleton = draw_cluster_skeleton(jax.random.fold_in(streams_of[11], 71), 0)
    return {"points": points, "charges": charges, "near_list": near_list, "near_count": near_count, "leaf_basis": leaf_basis, "device_basis": device_basis, "device_skeleton": device_skeleton, "group_basis": group_basis, "group_skeleton": group_skeleton, "cluster_basis": cluster_basis, "cluster_skeleton": cluster_skeleton}


inverse_spread = 1.0 / 16.0
exact_mode = lax.Precision.HIGHEST


def kernel_of(left_points, right_points):
    cross_terms = jnp.dot(left_points.T, right_points, precision=exact_mode, preferred_element_type=jnp.float32)
    left_square = jnp.sum(left_points * left_points, axis=0)
    right_square = jnp.sum(right_points * right_points, axis=0)
    return jnp.exp(-(left_square[:, None] + right_square[None, :] - 2.0 * cross_terms) * inverse_spread)


def near_field(points, charges, near_list, near_count):
    def per_leaf(leaf_index):
        start = (leaf_index * LEAF).astype(jnp.int32)
        target = lax.dynamic_slice_in_dim(points, start, LEAF, 1)

        def add_tile(slot_index, running):
            other = (near_list[leaf_index, slot_index] * LEAF).astype(jnp.int32)
            source = lax.dynamic_slice_in_dim(points, other, LEAF, 1)
            source_charges = lax.dynamic_slice_in_dim(charges, other, LEAF, 1).astype(jnp.bfloat16)
            kernel_tile = kernel_of(target, source).astype(jnp.bfloat16)
            return running + lax.dot_general(source_charges, kernel_tile, (((1,), (1,)), ((), ())), preferred_element_type=jnp.float32)

        return lax.fori_loop(0, near_count[leaf_index], add_tile, jnp.zeros((R, LEAF), jnp.float32))

    blocks = lax.map(per_leaf, jnp.arange(NLEAVES, dtype=jnp.int32))
    return jnp.transpose(blocks, (1, 0, 2)).reshape(R, NLEAVES * LEAF)


def pick_columns(values, indices):
    full_index = jnp.broadcast_to(indices[None], (values.shape[0],) + indices.shape)
    return jnp.take_along_axis(values, full_index, axis=2)


def reference(points, charges, near_list, near_count, leaf_basis, device_basis, device_skeleton, group_basis, group_skeleton, cluster_basis, cluster_skeleton):
    near = near_field(points, charges, near_list, near_count)
    device_total = NLEAVES // LEAVES_DEV
    group_total = device_total // 4
    cluster_total = device_total // 16
    points_each = LEAVES_DEV * LEAF
    leaf_blocks = leaf_basis.reshape(NLEAVES, LEAF, S)
    leaf_weights = jnp.einsum('lps,rlp->rls', leaf_blocks, charges.reshape(R, NLEAVES, LEAF), precision=exact_mode)
    device_blocks = device_basis.reshape(device_total, LEAVES_DEV * S, S)
    device_weights = jnp.einsum('dks,rdk->rds', device_blocks, leaf_weights.reshape(R, device_total, LEAVES_DEV * S), precision=exact_mode)
    device_points = pick_columns(points.reshape(F, device_total, points_each), device_skeleton)
    group_blocks = group_basis.reshape(4 * S, group_total, S)
    group_weights = jnp.einsum('kgs,rgk->rgs', group_blocks, device_weights.reshape(R, group_total, 4 * S), precision=exact_mode)
    group_points = pick_columns(device_points.reshape(F, group_total, 4 * S), group_skeleton.reshape(group_total, S))
    cluster_blocks = cluster_basis.reshape(4 * S, cluster_total, S)
    cluster_weights = jnp.einsum('kgs,rgk->rgs', cluster_blocks, group_weights.reshape(R, cluster_total, 4 * S), precision=exact_mode)
    cluster_points = pick_columns(group_points.reshape(F, cluster_total, 4 * S), cluster_skeleton.reshape(cluster_total, S))
    flat_points = cluster_points.reshape(F, cluster_total * S)
    flat_weights = cluster_weights.reshape(R, cluster_total * S)
    cluster_of = jnp.arange(cluster_total * S) // S
    top_kernel = kernel_of(flat_points, flat_points) * (cluster_of[:, None] != cluster_of[None, :])
    top = jnp.dot(flat_weights, top_kernel.T, precision=exact_mode)
    child_of = jnp.arange(4 * S) // S
    sibling_mask = child_of[:, None] != child_of[None, :]

    def side_of(pair):
        block_points, block_weights = pair
        return jnp.dot(block_weights, (kernel_of(block_points, block_points) * sibling_mask).T, precision=exact_mode)

    side_parts = lax.map(side_of, (jnp.moveaxis(group_points.reshape(F, cluster_total, 4 * S), 1, 0), jnp.moveaxis(group_weights.reshape(R, cluster_total, 4 * S), 1, 0)))
    side = jnp.moveaxis(side_parts, 0, 1).reshape(R, group_total, S)
    from_top = jnp.einsum('kgs,rgs->rgk', cluster_blocks, top.reshape(R, cluster_total, S), precision=exact_mode)
    down_group = side + from_top.reshape(R, group_total, S)
    down_device = jnp.einsum('kgs,rgs->rgk', group_blocks, down_group, precision=exact_mode).reshape(R, device_total, S)
    down_leaf = jnp.einsum('dks,rds->rdk', device_blocks, down_device, precision=exact_mode).reshape(R, NLEAVES, S)
    far_field = jnp.einsum('lps,rls->rlp', leaf_blocks, down_leaf, precision=exact_mode).reshape(R, NPTS)
    return near + far_field
```

```python
import functools

import jax
import jax.numpy as jnp
from jax import lax
from jax.experimental import pallas as pl
from jax.experimental.pallas import tpu as pltpu
from jax.sharding import PartitionSpec as P

F = 16
R = 16
LEAF = 512
S = 256
NBR = 32
LEAVES_DEV = 4
PTS = LEAVES_DEV * LEAF
INFO = 128
SKEL_LANE = 68
POINT_SCALE = 0.42466090014400953
UNROLL = 4
MAX_WORK = 16 * NBR + 16

f32 = jnp.float32
bf16 = jnp.bfloat16

NN = (((1,), (0,)), ((), ()))
NT = (((1,), (1,)), ((), ()))


def partner(value, mask):
    size = lax.axis_size("leaf")
    return lax.ppermute(value, "leaf", [(source, source ^ mask) for source in range(size)])


def shifted(value, steps):
    size = lax.axis_size("leaf")
    return lax.ppermute(
        value,
        "leaf",
        [(source, source + steps) for source in range(max(0, -steps), min(size, size - steps))],
    )


def call(body, outs, name, smem=(), n_in=0, scratch=()):
    specs = [
        pl.BlockSpec(memory_space=pltpu.SMEM if i in smem else pltpu.VMEM) for i in range(n_in)
    ]
    return pl.pallas_call(
        body,
        out_shape=outs,
        in_specs=specs,
        out_specs=jax.tree.map(lambda _: pl.BlockSpec(memory_space=pltpu.VMEM), outs),
        scratch_shapes=list(scratch),
        name=name,
    )


def out(*shape):
    return jax.ShapeDtypeStruct(shape, f32)


def split2(x):
    high = x.astype(bf16)
    return high, (x - high.astype(f32)).astype(bf16)


def split3(x):
    high = x.astype(bf16)
    rest = x - high.astype(f32)
    middle = rest.astype(bf16)
    return high, middle, (rest - middle.astype(f32)).astype(bf16)


def dot(a, b, dims):
    return lax.dot_general(a, b, dims, preferred_element_type=f32)


def product(a, b, dims):
    ah, al = split2(a)
    bh, bl = split2(b)
    rows = a.shape[0]
    both = dot(jnp.concatenate([ah, al], 0), bh, dims)
    return both[:rows] + both[rows:] + dot(ah, bl, dims)


def pick(points, one_hot, dims):
    parts = dot(jnp.concatenate(split3(points), 0), one_hot, dims)
    return parts[:F] + parts[F : 2 * F] + parts[2 * F :]


def one_hot_rows(index_column, first, width):
    lanes = lax.broadcasted_iota(jnp.int32, (index_column.shape[0], width), 1)
    return jnp.where(lanes + first == index_column.astype(jnp.int32), 1.0, 0.0).astype(bf16)


def exponent_rows(points, left):
    scaled = points * POINT_SCALE
    h, m, l = split3(scaled)
    n = points.shape[1]
    nh, nm, nl = split3(-0.5 * jnp.sum(scaled * scaled, axis=0, keepdims=True))
    row = lax.broadcasted_iota(jnp.int32, (16, n), 0)
    first = 0 if left else 3
    block = jnp.where((row >= 3 - first) & (row < 6 - first), 1.0, 0.0)
    for i, part in enumerate((nh, nm, nl)):
        block = jnp.where(row == first + i, part.astype(f32), block)
    block = block.astype(bf16)
    zero = jnp.zeros((16, n), bf16)
    if left:
        return jnp.concatenate([h, h, m, m, h, l, block, zero], 0)
    return jnp.concatenate([h, m, h, m, l, h, block, zero], 0)


def pack_first(points, charges, near_list, near_count, gskel, cskel, gbt, cbt, w, x1, c1, ckeep, csend):
    d = lax.axis_index("leaf")
    pos = d & 3
    gk = (d >> 2) & 3
    w[:F] = points[...]
    w[F:] = charges[...]
    x1[:, :PTS] = points[...]
    x1[:, PTS : PTS + INFO] = jnp.zeros((F, INFO), f32)
    x1[:4, PTS : PTS + NBR] = near_list[...].astype(f32)
    x1[:4, PTS + NBR : PTS + NBR + 1] = near_count[...].astype(f32)
    x1[:, PTS + SKEL_LANE : PTS + SKEL_LANE + 4] = gskel[...].astype(f32)
    for b, mask in enumerate((1, 3)):
        lane = pl.multiple_of((pos ^ mask) * S, S)
        for j in range(4):
            at = PTS + INFO + b * 4 * S + j * S
            x1[:, at : at + S] = gbt[16 * j : 16 * j + 16, pl.ds(lane, S)]
    for ref, row, mask in ((c1, 0, 2), (c1, 16, 3), (ckeep, 0, 0), (csend, 0, 1)):
        lane = pl.multiple_of((gk ^ mask) * S, S)
        ref[row : row + 16, :S] = cbt[:, pl.ds(lane, S)]
        ref[row : row + 16, S:] = jnp.broadcast_to(cskel[...].astype(f32), (16, INFO))


def pack_second(x1, x1r, gbt, x2):
    pos = lax.axis_index("leaf") & 3
    span = PTS + INFO
    x2[:, :span] = x1[:, :span]
    x2[:, span : 2 * span] = x1r[:, :span]
    lane = pl.multiple_of((pos ^ 2) * S, S)
    for j in range(4):
        at = 2 * span + j * S
        x2[:, at : at + S] = gbt[16 * j : 16 * j + 16, pl.ds(lane, S)]
    x2[:, 2 * span + 4 * S :] = x1r[:, span + 4 * S :]


def device_up(points, charges, leaf_basis, device_basis, skeleton, pay):
    rows = lax.broadcasted_iota(jnp.int32, (PTS, S), 0)
    one_hot = jnp.where(rows == skeleton[...], 1.0, 0.0).astype(bf16)
    pay[:F] = pick(points[...], one_hot, NN)
    total = jnp.zeros((R, S), f32)
    for l in range(LEAVES_DEV):
        weights = product(
            charges[:, l * LEAF : (l + 1) * LEAF], leaf_basis[l * LEAF : (l + 1) * LEAF], NN
        )
        total += product(weights, device_basis[l * S : (l + 1) * S], NN)
    pay[F:] = total


def group_up(pay, x1, x1r, x2r, gbt, part, rgbt, skel):
    pos = lax.axis_index("leaf") & 3
    span = PTS + INFO
    sources = (
        (0, None, 0, x1, PTS),
        (1, x1r, span, x1r, PTS),
        (2, x2r, 2 * span, x2r, PTS),
        (3, x2r, 2 * span + 4 * S, x2r, span + PTS),
    )
    for mask, ref, at, info, info_at in sources:
        first = (pos ^ mask) * 64
        for j in range(4):
            row = pl.multiple_of(first + 16 * j, 16)
            if ref is None:
                block = gbt[16 * j : 16 * j + 16, pl.ds(pl.multiple_of(pos * S, S), S)]
            else:
                block = ref[:, at + j * S : at + (j + 1) * S]
            rgbt[pl.ds(row, 16), :] = block
            lane = info_at + SKEL_LANE + j
            skel[pl.ds(row, 16), :] = jnp.broadcast_to(info[:, lane : lane + 1], (16, 128))
    part[:F] = pick(pay[:F], one_hot_rows(skel[:, :1], pos * S, S), NT)
    part[F:] = product(pay[F:], rgbt[...], NT)


CLUSTER_MASKS = (0, 8, 6, 14, 1, 9, 7, 15, 2, 10, 4, 12, 3, 11, 5, 13)


def cluster_up(gpay, c4, c4r, send, rcbt, skel):
    d = lax.axis_index("leaf")
    gk = (d >> 2) & 3
    for b, mask in enumerate(CLUSTER_MASKS):
        ref, at = (c4, 16 * b) if b < 8 else (c4r, 16 * b - 128)
        row = pl.multiple_of(((d & 15) ^ mask) * 16, 16)
        rcbt[pl.ds(row, 16), :] = ref[at : at + 16, :S]
        skel[pl.ds(row, 16), :] = ref[at : at + 16, S:]
    send[:, :S] = gpay[...]
    send[:F, S:] = pick(gpay[:F], one_hot_rows(skel[:, :1], gk * S, S), NT)
    send[F:, S:] = product(gpay[F:], rcbt[...], NT)


def interact(own_points, other_points, other_weights):
    left = jnp.transpose(exponent_rows(own_points, True))
    right = exponent_rows(other_points, False)
    values = jnp.exp2(dot(left, right, NN))
    return product(other_weights, values, NT)


def side_field(e2a, e2b, side):
    other_points = jnp.concatenate([e2a[:F, S : 2 * S], e2b[:F, : 2 * S]], 1)
    other_weights = jnp.concatenate([e2a[F:, S : 2 * S], e2b[F:, : 2 * S]], 1)
    side[...] = interact(e2a[:F, :S], other_points, other_weights)


def downward(e3b, r3, side, rcbt, rgbt, device_basis, leaf_basis, far):
    other_points = jnp.concatenate([e3b[:F, S:], r3[:F]], 1)
    other_weights = jnp.concatenate([e3b[F:, S:], r3[F:]], 1)
    top = interact(e3b[:F, :S], other_points, other_weights)
    down_group = side[...] + product(top, rcbt[...], NN)
    down_device = product(down_group, rgbt[...], NN)
    for l in range(LEAVES_DEV):
        down_leaf = product(down_device, device_basis[l * S : (l + 1) * S], NT)
        far[:, l * LEAF : (l + 1) * LEAF] = product(
            down_leaf, leaf_basis[l * LEAF : (l + 1) * LEAF], NT
        )


def near_field(info, w0, wm8, wm4, wp4, wp8, x1r, x2r, near_a, near_b, left, right, charge, acc, work):
    d = lax.axis_index("leaf")
    pos = d & 3

    def list_leaf(leaf, filled):
        def list_slot(slot, filled):
            source = info[leaf, slot]
            owner = source >> 2
            shard = (owner - d + 8) >> 2
            work[filled] = ((shard * 4 + (source & 3)) << 4) | leaf
            return filled + jnp.where((owner & 3) == pos, 1, 0)

        return lax.fori_loop(0, info[leaf, NBR], list_slot, filled)

    count = lax.fori_loop(0, 16, list_leaf, 0)

    for i, ref in enumerate((wm8, wm4, w0, wp4, wp8)):
        for l in range(LEAVES_DEV):
            cols = slice(l * LEAF, (l + 1) * LEAF)
            left[4 * i + l] = jnp.transpose(exponent_rows(ref[:F, cols], True))
            charge[4 * i + l] = ref[F:, cols].astype(bf16)
    span = PTS + INFO
    for q, (ref, at) in enumerate(((w0, 0), (x1r, 0), (x2r, 0), (x2r, span))):
        for l in range(LEAVES_DEV):
            right[4 * q + l] = exponent_rows(ref[:F, at + l * LEAF : at + (l + 1) * LEAF], False)
    acc[...] = jnp.zeros_like(acc)

    def tile(n):
        item = work[n]
        source = item >> 4
        target = item & 15
        values = jnp.exp2(dot(left[source], right[target], NN)).astype(bf16)
        acc[target] += dot(charge[source], values, NN)

    def several(step, _):
        for u in range(UNROLL):
            tile(step * UNROLL + u)
        return 0

    whole = count // UNROLL
    lax.fori_loop(0, whole, several, 0)

    def single(n, _):
        tile(n)
        return 0

    lax.fori_loop(whole * UNROLL, count, single, 0)
    for q in range(4):
        for l in range(LEAVES_DEV):
            ref = near_a if q < 2 else near_b
            ref[q & 1, :, l * LEAF : (l + 1) * LEAF] = acc[4 * q + l]


def shards(
    points,
    charges,
    near_list,
    near_count,
    leaf_basis,
    device_basis,
    device_skeleton,
    group_basis,
    group_skeleton,
    cluster_basis,
    cluster_skeleton,
):
    gbt = group_basis.T
    cbt = cluster_basis.T
    span = PTS + INFO
    w, x1, c1, ckeep, csend = call(
        pack_first,
        (out(32, PTS), out(16, span + 8 * S), out(32, S + INFO), out(16, S + INFO), out(16, S + INFO)),
        "pack_first",
        n_in=8,
    )(
        points,
        charges,
        near_list,
        near_count.reshape(4, 1),
        group_skeleton.reshape(4, 16).T,
        cluster_skeleton.reshape(16, 1),
        gbt,
        cbt,
    )
    x1r = partner(x1, 1)
    wm8 = shifted(w, 8)
    wp8 = shifted(w, -8)
    x2 = call(pack_second, out(16, 2 * span + 8 * S), "pack_second", n_in=3)(x1, x1r, gbt)
    x2r = partner(x2, 2)
    wm4 = shifted(w, 4)
    wp4 = shifted(w, -4)
    c1r = partner(c1, 8)
    c2r = partner(jnp.concatenate([csend, c1r[16:]], 0), 6)
    c3 = jnp.concatenate([ckeep, c1r[:16], c2r], 0)
    c4 = jnp.concatenate([c3, partner(c3, 1)], 0)
    c4r = partner(c4, 2)

    pay = call(device_up, out(32, S), "device_up", n_in=5)(
        points, charges, leaf_basis, device_basis, device_skeleton
    )
    part, rgbt, _ = call(group_up, (out(32, S), out(S, S), out(S, 128)), "group_up", n_in=5)(
        pay, x1, x1r, x2r, gbt
    )
    part = part + partner(part, 1)
    gpay = part + partner(part, 2)
    e2, rcbt, _ = call(cluster_up, (out(32, 2 * S), out(S, S), out(S, 128)), "cluster_up", n_in=3)(
        gpay, c4, c4r
    )
    e2r = partner(e2, 6)
    e2a = jnp.concatenate([e2[:, :S], e2r[:, :S], e2[:, S:] + e2r[:, S:]], 1)
    e2b = partner(e2a, 8)
    cpay = e2a[:, 2 * S :] + e2b[:, 2 * S :]
    e3a = jnp.concatenate([cpay, partner(cpay, 24)], 1)
    e3b = jnp.concatenate([e3a, partner(e3a, 32)], 1)
    r3 = partner(e3b, 96)
    side = call(side_field, out(16, S), "side_field", n_in=2)(e2a, e2b)

    info = jnp.concatenate(
        [
            x1[:4, PTS:span],
            x1r[:4, PTS:span],
            x2r[:4, PTS:span],
            x2r[:4, span + PTS : 2 * span],
        ],
        0,
    ).astype(jnp.int32)
    near_a, near_b = call(
        near_field,
        (out(2, 16, PTS), out(2, 16, PTS)),
        "near_field",
        smem=(0,),
        n_in=8,
        scratch=(
            pltpu.VMEM((20, LEAF, 128), bf16),
            pltpu.VMEM((16, 128, LEAF), bf16),
            pltpu.VMEM((20, R, LEAF), bf16),
            pltpu.VMEM((16, R, LEAF), f32),
            pltpu.SMEM((MAX_WORK,), jnp.int32),
        ),
    )(info, w, wm8, wm4, wp4, wp8, x1r, x2r)
    near_a = near_a + partner(near_b, 2)
    near = near_a[0] + partner(near_a[1], 1)
    far = call(downward, out(16, PTS), "downward", n_in=7)(
        e3b, r3, side, rcbt, rgbt, device_basis, leaf_basis
    )
    return near + far


def solution(mesh):
    return jax.shard_map(
        shards,
        mesh=mesh,
        in_specs=(
            P(None, "leaf"),
            P(None, "leaf"),
            P("leaf", None),
            P("leaf"),
            P("leaf", None),
            P("leaf", None),
            P("leaf", None),
            P(None, "leaf"),
            P("leaf"),
            P(None, "leaf"),
            P("leaf"),
        ),
        out_specs=P(None, "leaf"),
        check_vma=False,
    )
```

```python
import jax
import jax.numpy as jnp
from jax import lax
from jax.experimental import pallas as pl
from jax.experimental.pallas import tpu as pltpu
from jax.sharding import PartitionSpec as P


F = 16
R = 16
LEAF = 512
S = 256
NBR = 32
LEAVES_DEV = 4
PTS = LEAVES_DEV * LEAF
INFO = 128
SKEL_LANE = 68
POINT_SCALE = 0.42466090014400953
UNROLL = 4

f32 = jnp.float32
bf16 = jnp.bfloat16

NN = (((1,), (0,)), ((), ()))
NT = (((1,), (1,)), ((), ()))


def partner(value, mask):
    size = lax.axis_size("leaf")
    return lax.ppermute(value, "leaf", [(source, source ^ mask) for source in range(size)])


def staggered(value, step):
    size = lax.axis_size("leaf")
    pairs = [
        (source, (source + (step if source // step % 2 else -step)) % size)
        for source in range(size)
    ]
    return lax.ppermute(value, "leaf", pairs)


def call(body, outs, args, smem=(), hbm=(), scratch=(), smem_outs=(), aliases=None):
    spaces = [
        pltpu.SMEM if i in smem else pltpu.HBM if i in hbm else pltpu.VMEM
        for i in range(len(args))
    ]
    args = [
        pltpu.with_memory_space_constraint(arg, pltpu.HBM) if i in hbm else arg
        for i, arg in enumerate(args)
    ]
    return pl.pallas_call(
        body,
        out_shape=tuple(outs),
        in_specs=[pl.BlockSpec(memory_space=space) for space in spaces],
        out_specs=tuple(
            pl.BlockSpec(memory_space=pltpu.SMEM if i in smem_outs else pltpu.VMEM)
            for i in range(len(outs))
        ),
        input_output_aliases=aliases or {},
        scratch_shapes=list(scratch),
        compiler_params=pltpu.CompilerParams(vmem_limit_bytes=24 << 20),
    )(*args)


def out(*shape):
    return jax.ShapeDtypeStruct(shape, f32)


def split2(x):
    high = x.astype(bf16)
    return high, (x - high.astype(f32)).astype(bf16)


def split3(x):
    high = x.astype(bf16)
    rest = x - high.astype(f32)
    middle = rest.astype(bf16)
    return high, middle, (rest - middle.astype(f32)).astype(bf16)


def dot(a, b, dims):
    return lax.dot_general(a, b, dims, preferred_element_type=f32)


def product(a, b, dims):
    ah, al = split2(a)
    bh, bl = split2(b)
    rows = a.shape[0]
    both = dot(jnp.concatenate([ah, al], 0), bh, dims)
    return both[:rows] + both[rows:] + dot(ah, bl, dims)


def pick(points, one_hot, dims):
    parts = dot(jnp.concatenate(split3(points), 0), one_hot, dims)
    return parts[:F] + parts[F : 2 * F] + parts[2 * F :]


def one_hot_rows(index_column, first, width):
    lanes = lax.broadcasted_iota(jnp.int32, (index_column.shape[0], width), 1)
    return jnp.where(lanes + first == index_column.astype(jnp.int32), 1.0, 0.0).astype(bf16)


def exponent_rows(points, left):
    scaled = points * POINT_SCALE
    h, m, l = split3(scaled)
    n = points.shape[1]
    nh, nm, nl = split3(-0.5 * jnp.sum(scaled * scaled, axis=0, keepdims=True))
    row = lax.broadcasted_iota(jnp.int32, (16, n), 0)
    first = 0 if left else 3
    block = jnp.where((row >= 3 - first) & (row < 6 - first), 1.0, 0.0)
    for i, part in enumerate((nh, nm, nl)):
        block = jnp.where(row == first + i, part.astype(f32), block)
    block = block.astype(bf16)
    zero = jnp.zeros((16, n), bf16)
    if left:
        return jnp.concatenate([h, h, m, m, h, l, block, zero], 0)
    return jnp.concatenate([h, m, h, m, l, h, block, zero], 0)


SPAN = PTS + INFO
BLOCK = S + INFO


def cluster_block(ref, row, cbt, cskel, gk):
    ref[row : row + 16, :S] = cbt[:, pl.ds(pl.multiple_of(gk * S, S), S)]
    ref[row : row + 16, S:] = cskel


def skeleton_column(row_ref, count, tile):
    tile[...] = jnp.zeros((8, 128), f32)
    tile[0:1, :count] = row_ref[:, :count].astype(f32)
    return jnp.transpose(tile[...])


def pack_first(
    points, charges, near_list, near_count, gskel, cskel, gbt, cbt,
    w, w8, x1, urgent, gkeep, ckeep, csend,
    tile, lists, counts, grow, crow, group, cluster, sems,
):
    d = lax.axis_index("leaf")
    pos = d & 3
    gk = (d >> 2) & 3
    small = [
        pltpu.make_async_copy(source, target, sems.at[i])
        for i, (source, target) in enumerate(
            (
                (near_list, lists),
                (near_count, counts),
                (gskel, grow),
                (cskel, crow),
                (gbt, group),
                (cbt, cluster),
            )
        )
    ]
    cols = pl.ds(0, PTS)
    large = [
        pltpu.make_async_copy(source, target, sems.at[6 + i])
        for i, (source, target) in enumerate(
            (
                (points, w.at[pl.ds(0, F)]),
                (charges, w.at[pl.ds(F, R)]),
                (points, w8.at[pl.ds(0, F), cols]),
                (charges, w8.at[pl.ds(F, R), cols]),
                (points, x1.at[:, cols]),
            )
        )
    ]
    for copy in small + large:
        copy.start()
    x1[:, PTS:SPAN] = jnp.zeros((F, INFO), f32)
    for copy in small:
        copy.wait()
    x1[:4, PTS : PTS + NBR] = lists[...].astype(f32)
    for l in range(LEAVES_DEV):
        x1[l : l + 1, PTS + NBR : PTS + NBR + 1] = jnp.full((1, 1), counts[l], jnp.int32).astype(f32)
    column = skeleton_column(grow, 64, tile)
    for j in range(4):
        lane = PTS + SKEL_LANE + j
        x1[:, lane : lane + 1] = column[16 * j : 16 * j + 16, :1]
    for ref, start, mask in ((x1, SPAN, 1), (x1, SPAN + 4 * S, 3), (gkeep, 0, 0), (urgent, 0, 2)):
        lane = pl.multiple_of((pos ^ mask) * S, S)
        for j in range(4):
            at = start + j * S
            ref[:, at : at + S] = group[16 * j : 16 * j + 16, pl.ds(lane, S)]
    column = jnp.broadcast_to(skeleton_column(crow, 16, tile)[:16, :1], (16, INFO))
    for half, mask in ((0, 2), (16, 3)):
        lane = pl.multiple_of((gk ^ mask) * S, S)
        w8[half : half + 16, PTS : PTS + S] = cluster[:, pl.ds(lane, S)]
        w8[half : half + 16, PTS + S :] = column
    cluster_block(ckeep, 0, cluster, column, gk)
    cluster_block(csend, 0, cluster, column, gk ^ 1)
    for copy in large:
        copy.wait()


def device_up(w, leaf_hbm, device_hbm, skeleton, pay, leaf, device, sems):
    copies = []
    for l in range(LEAVES_DEV):
        rows = pl.ds(l * LEAF, LEAF)
        copies.append(pltpu.make_async_copy(leaf_hbm.at[rows], leaf.at[rows], sems.at[l]))
    last = pltpu.make_async_copy(device_hbm, device, sems.at[LEAVES_DEV])
    for copy in copies:
        copy.start()
    last.start()
    rows = lax.broadcasted_iota(jnp.int32, (PTS, S), 0)
    one_hot = jnp.where(rows == skeleton[...], 1.0, 0.0).astype(bf16)
    pay[:F] = pick(w[:F], one_hot, NN)
    weights = []
    for l in range(LEAVES_DEV):
        copies[l].wait()
        weights.append(
            product(w[F:, l * LEAF : (l + 1) * LEAF], leaf[l * LEAF : (l + 1) * LEAF], NN)
        )
    last.wait()
    pay[F:] = product(jnp.concatenate(weights, 1), device[...], NN)


def group_up(pay, x1, x1r, urgent, gkeep, ckeep, w8r, c2r, e1, rgbt, skel):
    pos = lax.axis_index("leaf") & 3
    sources = (
        (0, gkeep, 0, x1, PTS),
        (1, x1r, SPAN, x1r, PTS),
        (2, urgent, 0, urgent, 8 * S),
        (3, urgent, 4 * S, urgent, 8 * S + INFO),
    )
    for mask, ref, at, info, info_at in sources:
        first = (pos ^ mask) * 64
        for j in range(4):
            row = pl.multiple_of(first + 16 * j, 16)
            rgbt[pl.ds(row, 16), :] = ref[:, at + j * S : at + (j + 1) * S]
            lane = info_at + SKEL_LANE + j
            skel[pl.ds(row, 16), :] = jnp.broadcast_to(info[:, lane : lane + 1], (16, 128))
    e1[:F, :S] = pick(pay[:F], one_hot_rows(skel[:, :1], pos * S, S), NT)
    e1[F:32, :S] = product(pay[F:], rgbt[...], NT)
    e1[:32, S:] = jnp.zeros((32, INFO), f32)
    e1[32:48] = ckeep[...]
    e1[48:64] = w8r[:16, PTS:]
    e1[64:96] = c2r[...]


CLUSTER_MASKS = (0, 8, 6, 14)


def cluster_up(e1, r1, r2, r3, e2, rcbt, skel):
    d = lax.axis_index("leaf")
    gk = (d >> 2) & 3
    for m, ref in enumerate((e1, r1, r2, r3)):
        for b, mask in enumerate(CLUSTER_MASKS):
            row = pl.multiple_of(((d & 15) ^ mask ^ m) * 16, 16)
            rcbt[pl.ds(row, 16), :] = ref[32 + 16 * b : 48 + 16 * b, :S]
            skel[pl.ds(row, 16), :] = ref[32 + 16 * b : 48 + 16 * b, S:]
    group = e1[:32, :S] + r1[:32, :S] + (r2[:32, :S] + r3[:32, :S])
    e2[:, :S] = group
    e2[:F, S:] = pick(group[:F], one_hot_rows(skel[:, :1], gk * S, S), NT)
    e2[F:, S:] = product(group[F:], rcbt[...], NT)


def cluster_sum(e2, r1, r2, r3, cpay):
    cpay[...] = e2[:, S:] + r1[:, S:] + (r2[:, S:] + r3[:, S:])


def interact(left, other_points, other_weights):
    values = jnp.exp2(dot(left, exponent_rows(other_points, False), NN))
    return product(other_weights, values, NT)


def early_field(e2, g1, g2, g3, cpay, c1, c2, side, top):
    left = jnp.transpose(exponent_rows(e2[:F, :S], True))
    side[...] = interact(
        left,
        jnp.concatenate([g1[:F, :S], g2[:F, :S], g3[:F, :S]], 1),
        jnp.concatenate([g1[F:, :S], g2[F:, :S], g3[F:, :S]], 1),
    )
    left = jnp.transpose(exponent_rows(cpay[:F], True))
    top[...] = interact(
        left, jnp.concatenate([c1[:F], c2[:F]], 1), jnp.concatenate([c1[F:], c2[F:]], 1)
    )


def downward(cpay, c3, side, top, rcbt, rgbt, device, leaf, far):
    left = jnp.transpose(exponent_rows(cpay[:F], True))
    total = top[...] + interact(left, c3[:F], c3[F:])
    down_group = side[...] + product(total, rcbt[...], NN)
    down_device = product(down_group, rgbt[...], NN)
    down_leaves = product(down_device, device[...], NT)
    for l in range(LEAVES_DEV):
        far[:, l * LEAF : (l + 1) * LEAF] = product(
            down_leaves[:, l * S : (l + 1) * S], leaf[l * LEAF : (l + 1) * LEAF], NT
        )


def make_work(info, work, place):
    d = lax.axis_index("leaf")
    pos = d & 3
    even8 = 1 - ((d >> 3) & 1)
    even4 = 1 - ((d >> 2) & 1)
    place[0] = 1 + even8
    place[1] = 3 + even4
    place[2] = 0
    place[3] = 4 - even4
    place[4] = 2 - even8

    def list_leaf(leaf, filled):
        def list_slot(slot, filled):
            source = info[leaf, slot]
            owner = source >> 2
            mine = (owner & 3) == pos
            shard = place[jnp.where(mine, (owner - d + 8) >> 2, 0)]
            work[filled] = ((shard * 4 + (source & 3)) << 4) | leaf
            return filled + jnp.where(mine, 1, 0)

        return lax.fori_loop(0, info[leaf, NBR], list_slot, filled)

    return lax.fori_loop(0, 16, list_leaf, 0)


def run_tiles(first, last, work, left, right, charge, acc):
    def tile(n):
        item = work[n]
        source = item >> 4
        target = item & 15
        values = jnp.exp2(dot(left[source], right[target], NN)).astype(bf16)
        acc[target] += dot(charge[source], values, NN)

    def several(step, _):
        for u in range(UNROLL):
            tile(first + step * UNROLL + u)
        return 0

    whole = (last - first) // UNROLL
    lax.fori_loop(0, whole, several, 0)

    def single(n, _):
        tile(n)
        return 0

    lax.fori_loop(first + whole * UNROLL, last, single, 0)


PARTS = (0, 6, 11, 16)


def bounds(count, part):
    first = ((count * PARTS[part]) >> 4) & -UNROLL
    last = (count * PARTS[part + 1]) >> 4
    return first, last if part == len(PARTS) - 2 else last & -UNROLL


def near_start(info, w, w8, i8, w4, i4, x1r, targets, acc, left, right, charge, work, place):
    count = make_work(info, work, place)
    work[WORK - 1] = count
    for i, ref in enumerate((w, w8, i8, w4, i4)):
        for l in range(LEAVES_DEV):
            cols = slice(l * LEAF, (l + 1) * LEAF)
            left[4 * i + l] = jnp.transpose(exponent_rows(ref[:F, cols], True))
            charge[4 * i + l] = ref[F:, cols].astype(bf16)
    for q, (ref, at) in enumerate(((w, 0), (x1r, 0), (targets, 0), (targets, SPAN))):
        for l in range(LEAVES_DEV):
            right[4 * q + l] = exponent_rows(ref[:F, at + l * LEAF : at + (l + 1) * LEAF], False)
    acc[...] = jnp.zeros_like(acc)
    run_tiles(*bounds(count, 0), work, left, right, charge, acc)


def near_more(part):
    def body(work, left, right, charge, before, acc):
        del before
        run_tiles(*bounds(work[WORK - 1], part), work, left, right, charge, acc)

    return body


def near_last(work, left, right, charge, before, *parts_acc):
    *parts, acc = parts_acc
    acc[...] = before[...]
    run_tiles(*bounds(work[WORK - 1], len(PARTS) - 2), work, left, right, charge, acc)
    for q, part in enumerate(parts):
        for l in range(LEAVES_DEV):
            part[:, l * LEAF : (l + 1) * LEAF] = acc[4 * q + l]


WORK = 16 * NBR + 16


def program(
    points,
    charges,
    near_list,
    near_count,
    leaf_basis,
    device_basis,
    device_skeleton,
    group_basis,
    group_skeleton,
    cluster_basis,
    cluster_skeleton,
):
    w, w8, x1, urgent, gkeep, ckeep, csend = call(
        pack_first,
        (
            out(32, PTS),
            out(32, PTS + BLOCK),
            out(16, SPAN + 8 * S),
            out(16, 4 * S),
            out(16, 4 * S),
            out(16, BLOCK),
            out(16, BLOCK),
        ),
        (
            points,
            charges,
            near_list,
            near_count,
            group_skeleton.reshape(1, 64),
            cluster_skeleton.reshape(1, 16),
            group_basis.T,
            cluster_basis.T,
        ),
        hbm=range(8),
        scratch=(
            pltpu.VMEM((8, 128), f32),
            pltpu.VMEM((LEAVES_DEV, NBR), jnp.int32),
            pltpu.SMEM((LEAVES_DEV,), jnp.int32),
            pltpu.VMEM((1, 64), jnp.int32),
            pltpu.VMEM((1, 16), jnp.int32),
            pltpu.VMEM((64, 4 * S), f32),
            pltpu.VMEM((16, 4 * S), f32),
            pltpu.SemaphoreType.DMA((11,)),
        ),
    )
    x1r = partner(x1, 1)
    w4r = partner(w, 4)
    w8r = partner(w8, 8)
    i8r = staggered(w, 8)
    i4r = staggered(w, 4)
    urgent = jnp.concatenate([urgent, x1r[:, SPAN + 4 * S :], x1[:, PTS:SPAN], x1r[:, PTS:SPAN]], 1)
    targets = jnp.concatenate([x1[:, :SPAN], x1r[:, :SPAN]], 1)
    urgent = partner(urgent, 2)
    targets = partner(targets, 2)
    (pay,) = call(
        device_up,
        (out(32, S),),
        (w, leaf_basis, device_basis, device_skeleton),
        hbm=(1, 2),
        scratch=(
            pltpu.VMEM((PTS, S), f32),
            pltpu.VMEM((LEAVES_DEV * S, S), f32),
            pltpu.SemaphoreType.DMA((LEAVES_DEV + 1,)),
        ),
    )
    c2r = partner(jnp.concatenate([csend, w8r[16:, PTS:]], 0), 6)
    e1, rgbt, _ = call(
        group_up,
        (out(96, BLOCK), out(S, S), out(S, 128)),
        (pay, x1, x1r, urgent, gkeep, ckeep, w8r, c2r),
    )
    g1, g2, g3 = (partner(e1, m) for m in (1, 2, 3))
    e2, rcbt, _ = call(cluster_up, (out(32, 2 * S), out(S, S), out(S, 128)), (e1, g1, g2, g3))
    h1, h2, h3 = (partner(e2, m) for m in (8, 6, 14))
    (cpay,) = call(cluster_sum, (out(32, S),), (e2, h1, h2, h3))
    c1 = partner(cpay, 24)
    pair = jnp.concatenate([cpay, c1], 1)
    c2 = partner(pair, 32)
    c3 = partner(jnp.concatenate([pair, c2], 1), 96)
    side, top = call(early_field, (out(16, S), out(16, S)), (e2, h1, h2, h3, cpay, c1, c2))

    info = jnp.concatenate(
        [
            x1[:4, PTS:SPAN],
            x1r[:4, PTS:SPAN],
            targets[:4, PTS:SPAN],
            targets[:4, SPAN + PTS :],
        ],
        0,
    ).astype(jnp.int32)
    acc, left, right, charge, work = call(
        near_start,
        (
            out(16, R, LEAF),
            jax.ShapeDtypeStruct((20, LEAF, 128), bf16),
            jax.ShapeDtypeStruct((16, 128, LEAF), bf16),
            jax.ShapeDtypeStruct((20, R, LEAF), bf16),
            jax.ShapeDtypeStruct((WORK,), jnp.int32),
        ),
        (info, w, w8r, i8r, w4r, i4r, x1r, targets),
        smem=(0,),
        smem_outs=(4,),
        scratch=(pltpu.SMEM((8,), jnp.int32),),
    )
    for part in range(1, len(PARTS) - 2):
        (acc,) = call(
            near_more(part),
            (out(16, R, LEAF),),
            (work, left, right, charge, acc),
            smem=(0,),
            aliases={4: 0},
        )
    n0, n1, n2, n3 = call(
        near_last,
        (out(R, PTS),) * 4,
        (work, left, right, charge, acc),
        smem=(0,),
        scratch=(pltpu.VMEM((16, R, LEAF), f32),),
    )
    n3 = partner(n3, 3)
    n2 = partner(n2, 2)
    n1 = partner(n1, 1)
    (far,) = call(
        downward, (out(16, PTS),), (cpay, c3, side, top, rcbt, rgbt, device_basis, leaf_basis)
    )
    return n0 + n1 + (n2 + n3) + far


def solution(mesh):
    return jax.shard_map(
        program,
        mesh=mesh,
        in_specs=(
            P(None, "leaf"),
            P(None, "leaf"),
            P("leaf", None),
            P("leaf"),
            P("leaf", None),
            P("leaf", None),
            P("leaf", None),
            P(None, "leaf"),
            P("leaf"),
            P(None, "leaf"),
            P("leaf"),
        ),
        out_specs=P(None, "leaf"),
        check_vma=False,
    )
```

```python
import jax
import jax.numpy as jnp
from jax import lax
from jax.experimental import pallas as pl
from jax.experimental.pallas import tpu as pltpu
from jax.sharding import PartitionSpec as P


F = 16
R = 16
LEAF = 512
S = 256
NBR = 32
LEAVES_DEV = 4
PTS = LEAVES_DEV * LEAF
INFO = 128
SKEL_LANE = 68
POINT_SCALE = 0.42466090014400953
UNROLL = 4

f32 = jnp.float32
bf16 = jnp.bfloat16

NN = (((1,), (0,)), ((), ()))
NT = (((1,), (1,)), ((), ()))


def partner(value, mask):
    size = lax.axis_size("leaf")
    return lax.ppermute(value, "leaf", [(source, source ^ mask) for source in range(size)])


def staggered(value, step):
    size = lax.axis_size("leaf")
    pairs = [
        (source, (source + (step if source // step % 2 else -step)) % size)
        for source in range(size)
    ]
    return lax.ppermute(value, "leaf", pairs)


def call(body, outs, args, smem=(), hbm=(), scratch=(), smem_outs=(), aliases=None):
    spaces = [
        pltpu.SMEM if i in smem else pltpu.HBM if i in hbm else pltpu.VMEM
        for i in range(len(args))
    ]
    args = [
        pltpu.with_memory_space_constraint(arg, pltpu.HBM) if i in hbm else arg
        for i, arg in enumerate(args)
    ]
    return pl.pallas_call(
        body,
        out_shape=tuple(outs),
        in_specs=[pl.BlockSpec(memory_space=space) for space in spaces],
        out_specs=tuple(
            pl.BlockSpec(memory_space=pltpu.SMEM if i in smem_outs else pltpu.VMEM)
            for i in range(len(outs))
        ),
        input_output_aliases=aliases or {},
        scratch_shapes=list(scratch),
        compiler_params=pltpu.CompilerParams(vmem_limit_bytes=24 << 20),
    )(*args)


def out(*shape):
    return jax.ShapeDtypeStruct(shape, f32)


def split2(x):
    high = x.astype(bf16)
    return high, (x - high.astype(f32)).astype(bf16)


def split3(x):
    high = x.astype(bf16)
    rest = x - high.astype(f32)
    middle = rest.astype(bf16)
    return high, middle, (rest - middle.astype(f32)).astype(bf16)


def dot(a, b, dims):
    return lax.dot_general(a, b, dims, preferred_element_type=f32)


def product(a, b, dims):
    ah, al = split2(a)
    bh, bl = split2(b)
    rows = a.shape[0]
    both = dot(jnp.concatenate([ah, al], 0), bh, dims)
    return both[:rows] + both[rows:] + dot(ah, bl, dims)


def pick(points, one_hot, dims):
    parts = dot(jnp.concatenate(split3(points), 0), one_hot, dims)
    return parts[:F] + parts[F : 2 * F] + parts[2 * F :]


def one_hot_rows(index_column, first, width):
    lanes = lax.broadcasted_iota(jnp.int32, (index_column.shape[0], width), 1)
    return jnp.where(lanes + first == index_column.astype(jnp.int32), 1.0, 0.0).astype(bf16)


def exponent_rows(points, left):
    scaled = points * POINT_SCALE
    h, m, l = split3(scaled)
    n = points.shape[1]
    nh, nm, nl = split3(-0.5 * jnp.sum(scaled * scaled, axis=0, keepdims=True))
    row = lax.broadcasted_iota(jnp.int32, (16, n), 0)
    first = 0 if left else 3
    block = jnp.where((row >= 3 - first) & (row < 6 - first), 1.0, 0.0)
    for i, part in enumerate((nh, nm, nl)):
        block = jnp.where(row == first + i, part.astype(f32), block)
    block = block.astype(bf16)
    zero = jnp.zeros((16, n), bf16)
    if left:
        return jnp.concatenate([h, h, m, m, h, l, block, zero], 0)
    return jnp.concatenate([h, m, h, m, l, h, block, zero], 0)


SPAN = PTS + INFO
BLOCK = S + INFO


def cluster_block(ref, row, cbt, cskel, gk):
    ref[row : row + 16, :S] = cbt[:, pl.ds(pl.multiple_of(gk * S, S), S)]
    ref[row : row + 16, S:] = cskel


def skeleton_column(row_ref, count, tile):
    tile[...] = jnp.zeros((8, 128), f32)
    tile[0:1, :count] = row_ref[:, :count].astype(f32)
    return jnp.transpose(tile[...])


def pack_first(
    points, charges, near_list, near_count, gskel, cskel, gbt, cbt,
    w, x1, urgent, gkeep, ckeep, csend, c1,
    tile, lists, counts, grow, crow, group, cluster, sems,
):
    d = lax.axis_index("leaf")
    pos = d & 3
    gk = (d >> 2) & 3
    small = [
        pltpu.make_async_copy(source, target, sems.at[i])
        for i, (source, target) in enumerate(
            (
                (near_list, lists),
                (near_count, counts),
                (gskel, grow),
                (cskel, crow),
                (gbt, group),
                (cbt, cluster),
            )
        )
    ]
    cols = pl.ds(0, PTS)
    large = [
        pltpu.make_async_copy(source, target, sems.at[6 + i])
        for i, (source, target) in enumerate(
            (
                (points, w.at[pl.ds(0, F)]),
                (charges, w.at[pl.ds(F, R)]),
                (points, x1.at[:, cols]),
            )
        )
    ]
    for copy in small + large:
        copy.start()
    x1[:, PTS:SPAN] = jnp.zeros((F, INFO), f32)
    for copy in small:
        copy.wait()
    x1[:4, PTS : PTS + NBR] = lists[...].astype(f32)
    for l in range(LEAVES_DEV):
        x1[l : l + 1, PTS + NBR : PTS + NBR + 1] = jnp.full((1, 1), counts[l], jnp.int32).astype(f32)
    column = skeleton_column(grow, 64, tile)
    for j in range(4):
        lane = PTS + SKEL_LANE + j
        x1[:, lane : lane + 1] = column[16 * j : 16 * j + 16, :1]
    for ref, start, mask in ((x1, SPAN, 1), (x1, SPAN + 4 * S, 3), (gkeep, 0, 0), (urgent, 0, 2)):
        lane = pl.multiple_of((pos ^ mask) * S, S)
        for j in range(4):
            at = start + j * S
            ref[:, at : at + S] = group[16 * j : 16 * j + 16, pl.ds(lane, S)]
    column = jnp.broadcast_to(skeleton_column(crow, 16, tile)[:16, :1], (16, INFO))
    cluster_block(c1, 0, cluster, column, gk ^ 2)
    cluster_block(c1, 16, cluster, column, gk ^ 3)
    cluster_block(ckeep, 0, cluster, column, gk)
    cluster_block(csend, 0, cluster, column, gk ^ 1)
    for copy in large:
        copy.wait()


def device_up(w, leaf_hbm, device_hbm, skeleton, pay, leaf, device, sems):
    copies = []
    for l in range(LEAVES_DEV):
        rows = pl.ds(l * LEAF, LEAF)
        copies.append(pltpu.make_async_copy(leaf_hbm.at[rows], leaf.at[rows], sems.at[l]))
    last = pltpu.make_async_copy(device_hbm, device, sems.at[LEAVES_DEV])
    for copy in copies:
        copy.start()
    last.start()
    rows = lax.broadcasted_iota(jnp.int32, (PTS, S), 0)
    one_hot = jnp.where(rows == skeleton[...], 1.0, 0.0).astype(bf16)
    pay[:F] = pick(w[:F], one_hot, NN)
    weights = []
    for l in range(LEAVES_DEV):
        copies[l].wait()
        weights.append(
            product(w[F:, l * LEAF : (l + 1) * LEAF], leaf[l * LEAF : (l + 1) * LEAF], NN)
        )
    last.wait()
    pay[F:] = product(jnp.concatenate(weights, 1), device[...], NN)


def group_up(pay, x1, x1r, urgent, gkeep, ckeep, c1r, c2r, e1, rgbt, skel):
    pos = lax.axis_index("leaf") & 3
    sources = (
        (0, gkeep, 0, x1, PTS),
        (1, x1r, SPAN, x1r, PTS),
        (2, urgent, 0, urgent, 8 * S),
        (3, urgent, 4 * S, urgent, 8 * S + INFO),
    )
    for mask, ref, at, info, info_at in sources:
        first = (pos ^ mask) * 64
        for j in range(4):
            row = pl.multiple_of(first + 16 * j, 16)
            rgbt[pl.ds(row, 16), :] = ref[:, at + j * S : at + (j + 1) * S]
            lane = info_at + SKEL_LANE + j
            skel[pl.ds(row, 16), :] = jnp.broadcast_to(info[:, lane : lane + 1], (16, 128))
    e1[:F, :S] = pick(pay[:F], one_hot_rows(skel[:, :1], pos * S, S), NT)
    e1[F:32, :S] = product(pay[F:], rgbt[...], NT)
    e1[:32, S:] = jnp.zeros((32, INFO), f32)
    e1[32:48] = ckeep[...]
    e1[48:64] = c1r[:16]
    e1[64:96] = c2r[...]


CLUSTER_MASKS = (0, 8, 6, 14)


def cluster_up(e1, r1, r2, r3, e2, rcbt, skel):
    d = lax.axis_index("leaf")
    gk = (d >> 2) & 3
    for m, ref in enumerate((e1, r1, r2, r3)):
        for b, mask in enumerate(CLUSTER_MASKS):
            row = pl.multiple_of(((d & 15) ^ mask ^ m) * 16, 16)
            rcbt[pl.ds(row, 16), :] = ref[32 + 16 * b : 48 + 16 * b, :S]
            skel[pl.ds(row, 16), :] = ref[32 + 16 * b : 48 + 16 * b, S:]
    group = e1[:32, :S] + r1[:32, :S] + (r2[:32, :S] + r3[:32, :S])
    e2[:, :S] = group
    e2[:F, S:] = pick(group[:F], one_hot_rows(skel[:, :1], gk * S, S), NT)
    e2[F:, S:] = product(group[F:], rcbt[...], NT)


def cluster_sum(e2, r1, r2, r3, cpay):
    cpay[...] = e2[:, S:] + r1[:, S:] + (r2[:, S:] + r3[:, S:])


def interact(left, other_points, other_weights):
    values = jnp.exp2(dot(left, exponent_rows(other_points, False), NN))
    return product(other_weights, values, NT)


def early_field(e2, g1, g2, g3, cpay, c1, c2, side, top):
    left = jnp.transpose(exponent_rows(e2[:F, :S], True))
    side[...] = interact(
        left,
        jnp.concatenate([g1[:F, :S], g2[:F, :S], g3[:F, :S]], 1),
        jnp.concatenate([g1[F:, :S], g2[F:, :S], g3[F:, :S]], 1),
    )
    left = jnp.transpose(exponent_rows(cpay[:F], True))
    top[...] = interact(
        left, jnp.concatenate([c1[:F], c2[:F]], 1), jnp.concatenate([c1[F:], c2[F:]], 1)
    )


def downward(cpay, c3, side, top, rcbt, rgbt, device, leaf, far):
    left = jnp.transpose(exponent_rows(cpay[:F], True))
    total = top[...] + interact(left, c3[:F], c3[F:])
    down_group = side[...] + product(total, rcbt[...], NN)
    down_device = product(down_group, rgbt[...], NN)
    down_leaves = product(down_device, device[...], NT)
    for l in range(LEAVES_DEV):
        far[:, l * LEAF : (l + 1) * LEAF] = product(
            down_leaves[:, l * S : (l + 1) * S], leaf[l * LEAF : (l + 1) * LEAF], NT
        )


def make_work(info, work, place):
    d = lax.axis_index("leaf")
    pos = d & 3
    even8 = 1 - ((d >> 3) & 1)
    even4 = 1 - ((d >> 2) & 1)
    place[0] = 1 + even8
    place[1] = 3 + even4
    place[2] = 0
    place[3] = 4 - even4
    place[4] = 2 - even8

    def list_leaf(leaf, filled):
        live = info[leaf, NBR]

        def list_slots(step, filled):
            for u in range(4):
                slot = step * 4 + u
                source = info[leaf, slot]
                owner = source >> 2
                mine = ((owner & 3) == pos) & (slot < live)
                shard = place[jnp.where(mine, (owner - d + 8) >> 2, 0)]
                work[filled] = ((shard * 4 + (source & 3)) << 4) | leaf
                filled += jnp.where(mine, 1, 0)
            return filled

        return lax.fori_loop(0, (live + 3) >> 2, list_slots, filled)

    return lax.fori_loop(0, 16, list_leaf, 0)


def run_tiles(first, last, work, left, right, charge, acc):
    def tiles(start, number):
        items = [work[start + u] for u in range(number)]
        pairs = [(item >> 4, item & 15) for item in items]
        exponents = [dot(left[source], right[target], NN) for source, target in pairs]
        sums = [
            dot(charge[source], jnp.exp2(exponent).astype(bf16), NN)
            for (source, _), exponent in zip(pairs, exponents)
        ]
        for (_, target), total in zip(pairs, sums):
            acc[target] += total

    def several(step, _):
        tiles(first + step * UNROLL, UNROLL)
        return 0

    whole = (last - first) // UNROLL
    lax.fori_loop(0, whole, several, 0)

    def single(n, _):
        tiles(n, 1)
        return 0

    lax.fori_loop(first + whole * UNROLL, last, single, 0)


PARTS = (0, 5, 9, 13, 16)


def bounds(count, part):
    first = ((count * PARTS[part]) >> 4) & -UNROLL
    last = (count * PARTS[part + 1]) >> 4
    return first, last if part == len(PARTS) - 2 else last & -UNROLL


def source_rows(ref, shard, left, charge):
    for l in range(LEAVES_DEV):
        cols = slice(l * LEAF, (l + 1) * LEAF)
        left[4 * shard + l] = jnp.transpose(exponent_rows(ref[:F, cols], True))
        charge[4 * shard + l] = ref[F:, cols].astype(bf16)


def target_rows(ref, at, q, right):
    for l in range(LEAVES_DEV):
        right[4 * q + l] = exponent_rows(ref[:F, at + l * LEAF : at + (l + 1) * LEAF], False)


def near_plan(info, w, x1r, left, right, charge, work, place):
    count = make_work(info, work, place)
    work[WORK - 1] = count
    source_rows(w, 0, left, charge)
    target_rows(w, 0, 0, right)
    target_rows(x1r, 0, 1, right)


def near_start(work, w8, i8, w4, i4, targets, left0, right0, charge0, acc, left, right, charge):
    del left0, right0, charge0
    for i, ref in enumerate((w8, i8, w4, i4)):
        source_rows(ref, 1 + i, left, charge)
    for q in range(2):
        target_rows(targets, q * SPAN, 2 + q, right)
    acc[...] = jnp.zeros_like(acc)
    run_tiles(*bounds(work[WORK - 1], 0), work, left, right, charge, acc)


def near_more(part):
    def body(work, left, right, charge, before, acc):
        del before
        run_tiles(*bounds(work[WORK - 1], part), work, left, right, charge, acc)

    return body


def near_last(work, left, right, charge, before, *parts_acc):
    *parts, acc = parts_acc
    acc[...] = before[...]
    run_tiles(*bounds(work[WORK - 1], len(PARTS) - 2), work, left, right, charge, acc)
    for q, part in enumerate(parts):
        for l in range(LEAVES_DEV):
            part[:, l * LEAF : (l + 1) * LEAF] = acc[4 * q + l]


WORK = 16 * NBR + 16


def program(
    points,
    charges,
    near_list,
    near_count,
    leaf_basis,
    device_basis,
    device_skeleton,
    group_basis,
    group_skeleton,
    cluster_basis,
    cluster_skeleton,
):
    w, x1, urgent, gkeep, ckeep, csend, c1 = call(
        pack_first,
        (
            out(32, PTS),
            out(16, SPAN + 8 * S),
            out(16, 4 * S),
            out(16, 4 * S),
            out(16, BLOCK),
            out(16, BLOCK),
            out(32, BLOCK),
        ),
        (
            points,
            charges,
            near_list,
            near_count,
            group_skeleton.reshape(1, 64),
            cluster_skeleton.reshape(1, 16),
            group_basis.T,
            cluster_basis.T,
        ),
        hbm=range(8),
        scratch=(
            pltpu.VMEM((8, 128), f32),
            pltpu.VMEM((LEAVES_DEV, NBR), jnp.int32),
            pltpu.SMEM((LEAVES_DEV,), jnp.int32),
            pltpu.VMEM((1, 64), jnp.int32),
            pltpu.VMEM((1, 16), jnp.int32),
            pltpu.VMEM((64, 4 * S), f32),
            pltpu.VMEM((16, 4 * S), f32),
            pltpu.SemaphoreType.DMA((9,)),
        ),
    )
    x1r = partner(x1, 1)
    w4r = partner(w, 4)
    c1r = partner(c1, 8)
    w8r = partner(w, 8)
    i8r = staggered(w, 8)
    i4r = staggered(w, 4)
    urgent = jnp.concatenate([urgent, x1r[:, SPAN + 4 * S :], x1[:, PTS:SPAN], x1r[:, PTS:SPAN]], 1)
    targets = jnp.concatenate([x1[:, :SPAN], x1r[:, :SPAN]], 1)
    urgent = partner(urgent, 2)
    targets = partner(targets, 2)
    (pay,) = call(
        device_up,
        (out(32, S),),
        (w, leaf_basis, device_basis, device_skeleton),
        hbm=(1, 2),
        scratch=(
            pltpu.VMEM((PTS, S), f32),
            pltpu.VMEM((LEAVES_DEV * S, S), f32),
            pltpu.SemaphoreType.DMA((LEAVES_DEV + 1,)),
        ),
    )
    c2r = partner(jnp.concatenate([csend, c1r[16:]], 0), 6)
    e1, rgbt, _ = call(
        group_up,
        (out(96, BLOCK), out(S, S), out(S, 128)),
        (pay, x1, x1r, urgent, gkeep, ckeep, c1r, c2r),
    )
    g1, g2, g3 = (partner(e1, m) for m in (1, 2, 3))
    e2, rcbt, _ = call(cluster_up, (out(32, 2 * S), out(S, S), out(S, 128)), (e1, g1, g2, g3))
    h1, h2, h3 = (partner(e2, m) for m in (8, 6, 14))
    (cpay,) = call(cluster_sum, (out(32, S),), (e2, h1, h2, h3))
    c1 = partner(cpay, 24)
    pair = jnp.concatenate([cpay, c1], 1)
    c2 = partner(pair, 32)
    c3 = partner(jnp.concatenate([pair, c2], 1), 96)
    side, top = call(early_field, (out(16, S), out(16, S)), (e2, h1, h2, h3, cpay, c1, c2))

    info = jnp.concatenate(
        [
            x1[:4, PTS:SPAN],
            x1r[:4, PTS:SPAN],
            urgent[:4, 8 * S : 8 * S + INFO],
            urgent[:4, 8 * S + INFO :],
        ],
        0,
    ).astype(jnp.int32)
    rows = (
        jax.ShapeDtypeStruct((20, LEAF, 128), bf16),
        jax.ShapeDtypeStruct((16, 128, LEAF), bf16),
        jax.ShapeDtypeStruct((20, R, LEAF), bf16),
    )
    left, right, charge, work = call(
        near_plan,
        (*rows, jax.ShapeDtypeStruct((WORK,), jnp.int32)),
        (info, w, x1r),
        smem=(0,),
        smem_outs=(3,),
        scratch=(pltpu.SMEM((8,), jnp.int32),),
    )
    acc, left, right, charge = call(
        near_start,
        (out(16, R, LEAF), *rows),
        (work, w8r, i8r, w4r, i4r, targets, left, right, charge),
        smem=(0,),
        aliases={6: 1, 7: 2, 8: 3},
    )
    for part in range(1, len(PARTS) - 2):
        (acc,) = call(
            near_more(part),
            (out(16, R, LEAF),),
            (work, left, right, charge, acc),
            smem=(0,),
            aliases={4: 0},
        )
    n0, n1, n2, n3 = call(
        near_last,
        (out(R, PTS),) * 4,
        (work, left, right, charge, acc),
        smem=(0,),
        scratch=(pltpu.VMEM((16, R, LEAF), f32),),
    )
    n3 = partner(n3, 3)
    n2 = partner(n2, 2)
    n1 = partner(n1, 1)
    (far,) = call(
        downward, (out(16, PTS),), (cpay, c3, side, top, rcbt, rgbt, device_basis, leaf_basis)
    )
    return n0 + n1 + (n2 + n3) + far


def solution(mesh):
    return jax.shard_map(
        program,
        mesh=mesh,
        in_specs=(
            P(None, "leaf"),
            P(None, "leaf"),
            P("leaf", None),
            P("leaf"),
            P("leaf", None),
            P("leaf", None),
            P("leaf", None),
            P(None, "leaf"),
            P("leaf"),
            P(None, "leaf"),
            P("leaf"),
        ),
        out_specs=P(None, "leaf"),
        check_vma=False,
    )
```

```python
import jax
import jax.numpy as jnp
from jax import lax
from jax.experimental import pallas as pl
from jax.experimental.pallas import tpu as pltpu
from jax.sharding import PartitionSpec as P


F = 16
R = 16
LEAF = 512
S = 256
NBR = 32
LEAVES_DEV = 4
PTS = LEAVES_DEV * LEAF
INFO = 128
SKEL_LANE = 68
POINT_SCALE = 0.42466090014400953
UNROLL = 4

f32 = jnp.float32
bf16 = jnp.bfloat16

NN = (((1,), (0,)), ((), ()))
NT = (((1,), (1,)), ((), ()))


def partner(value, mask):
    size = lax.axis_size("leaf")
    return lax.ppermute(value, "leaf", [(source, source ^ mask) for source in range(size)])


def staggered(value, step):
    size = lax.axis_size("leaf")
    pairs = [
        (source, target if 0 <= target < size else source)
        for source, target in (
            (source, source + (step if source // step % 2 else -step)) for source in range(size)
        )
    ]
    return lax.ppermute(value, "leaf", pairs)


def call(body, outs, args, smem=(), hbm=(), scratch=(), smem_outs=(), aliases=None):
    spaces = [
        pltpu.SMEM if i in smem else pltpu.HBM if i in hbm else pltpu.VMEM
        for i in range(len(args))
    ]
    args = [
        pltpu.with_memory_space_constraint(arg, pltpu.HBM) if i in hbm else arg
        for i, arg in enumerate(args)
    ]
    return pl.pallas_call(
        body,
        out_shape=tuple(outs),
        in_specs=[pl.BlockSpec(memory_space=space) for space in spaces],
        out_specs=tuple(
            pl.BlockSpec(memory_space=pltpu.SMEM if i in smem_outs else pltpu.VMEM)
            for i in range(len(outs))
        ),
        input_output_aliases=aliases or {},
        scratch_shapes=list(scratch),
        compiler_params=pltpu.CompilerParams(vmem_limit_bytes=24 << 20),
    )(*args)


def out(*shape):
    return jax.ShapeDtypeStruct(shape, f32)


def split2(x):
    high = x.astype(bf16)
    return high, (x - high.astype(f32)).astype(bf16)


def split3(x):
    high = x.astype(bf16)
    rest = x - high.astype(f32)
    middle = rest.astype(bf16)
    return high, middle, (rest - middle.astype(f32)).astype(bf16)


def dot(a, b, dims):
    return lax.dot_general(a, b, dims, preferred_element_type=f32)


def product(a, b, dims):
    ah, al = split2(a)
    bh, bl = split2(b)
    rows = a.shape[0]
    both = dot(jnp.concatenate([ah, al], 0), bh, dims)
    return both[:rows] + both[rows:] + dot(ah, bl, dims)


def pick(points, one_hot, dims):
    parts = dot(jnp.concatenate(split3(points), 0), one_hot, dims)
    return parts[:F] + parts[F : 2 * F] + parts[2 * F :]


def one_hot_rows(index_column, first, width):
    lanes = lax.broadcasted_iota(jnp.int32, (index_column.shape[0], width), 1)
    return jnp.where(lanes + first == index_column.astype(jnp.int32), 1.0, 0.0).astype(bf16)


def exponent_rows(points, left):
    scaled = points * POINT_SCALE
    h, m, l = split3(scaled)
    n = points.shape[1]
    nh, nm, nl = split3(-0.5 * jnp.sum(scaled * scaled, axis=0, keepdims=True))
    row = lax.broadcasted_iota(jnp.int32, (16, n), 0)
    first = 0 if left else 3
    block = jnp.where((row >= 3 - first) & (row < 6 - first), 1.0, 0.0)
    for i, part in enumerate((nh, nm, nl)):
        block = jnp.where(row == first + i, part.astype(f32), block)
    block = block.astype(bf16)
    zero = jnp.zeros((16, n), bf16)
    if left:
        return jnp.concatenate([h, h, m, m, h, l, block, zero], 0)
    return jnp.concatenate([h, m, h, m, l, h, block, zero], 0)


SPAN = PTS + INFO
BLOCK = S + INFO


def skeleton_column(row_ref, count, tile):
    tile[...] = jnp.zeros((8, 128), f32)
    tile[0:1, :count] = row_ref[:, :count].astype(f32)
    return jnp.transpose(tile[...])


def pack_first(
    points, charges, near_list, near_count, gskel, cskel, gbt, cbt,
    w, x2, gnext, gkeep, ckeep, c8, c6, c14,
    tile, lists, counts, grow, crow, group, cluster, sems,
):
    d = lax.axis_index("leaf")
    pos = d & 3
    gk = (d >> 2) & 3
    small = [
        pltpu.make_async_copy(source, target, sems.at[i])
        for i, (source, target) in enumerate(
            (
                (near_list, lists),
                (near_count, counts),
                (gskel, grow),
                (cskel, crow),
                (gbt, group),
                (cbt, cluster),
            )
        )
    ]
    cols = pl.ds(0, PTS)
    large = [
        pltpu.make_async_copy(source, target, sems.at[6 + i])
        for i, (source, target) in enumerate(
            (
                (points, w.at[pl.ds(0, F)]),
                (charges, w.at[pl.ds(F, R)]),
                (points, x2.at[:, cols]),
            )
        )
    ]
    for copy in small + large:
        copy.start()
    x2[:, PTS:SPAN] = jnp.zeros((F, INFO), f32)
    for copy in small:
        copy.wait()
    x2[:4, PTS : PTS + NBR] = lists[...].astype(f32)
    for l in range(LEAVES_DEV):
        x2[l : l + 1, PTS + NBR : PTS + NBR + 1] = jnp.full((1, 1), counts[l], jnp.int32).astype(f32)
    column = skeleton_column(grow, 64, tile)
    for j in range(4):
        lane = PTS + SKEL_LANE + j
        x2[:, lane : lane + 1] = column[16 * j : 16 * j + 16, :1]
    for ref, start, mask in ((x2, SPAN, 2), (x2, SPAN + 4 * S, 3), (gkeep, 0, 0), (gnext, 0, 1)):
        lane = pl.multiple_of((pos ^ mask) * S, S)
        for j in range(4):
            at = start + j * S
            ref[:, at : at + S] = group[16 * j : 16 * j + 16, pl.ds(lane, S)]
    column = jnp.broadcast_to(skeleton_column(crow, 16, tile)[:16, :1], (16, INFO))
    for ref, mask in ((ckeep, 0), (c8, 2), (c6, 1), (c14, 3)):
        ref[:, :S] = cluster[:, pl.ds(pl.multiple_of((gk ^ mask) * S, S), S)]
        ref[:, S:] = column
    for copy in large:
        copy.wait()


def device_up(w, leaf_hbm, device_hbm, skeleton_hbm, pay, leaf, device, skeleton, sems):
    copies = []
    for l in range(LEAVES_DEV):
        rows = pl.ds(l * LEAF, LEAF)
        copies.append(pltpu.make_async_copy(leaf_hbm.at[rows], leaf.at[rows], sems.at[l]))
    last = pltpu.make_async_copy(device_hbm, device, sems.at[LEAVES_DEV])
    index = pltpu.make_async_copy(skeleton_hbm, skeleton, sems.at[LEAVES_DEV + 1])
    index.start()
    for copy in copies:
        copy.start()
    last.start()
    index.wait()
    rows = lax.broadcasted_iota(jnp.int32, (PTS, S), 0)
    one_hot = jnp.where(rows == skeleton[...], 1.0, 0.0).astype(bf16)
    pay[:F] = pick(w[:F], one_hot, NN)
    weights = []
    for l in range(LEAVES_DEV):
        copies[l].wait()
        weights.append(
            product(w[F:, l * LEAF : (l + 1) * LEAF], leaf[l * LEAF : (l + 1) * LEAF], NN)
        )
    last.wait()
    pay[F:] = product(jnp.concatenate(weights, 1), device[...], NN)


def group_up(pay, x2, x2r, x1r, gkeep, ckeep, c8, c6, c14, e1, rgbt, skel):
    pos = lax.axis_index("leaf") & 3
    sources = (
        (0, gkeep, 0, x2, PTS),
        (1, x1r, 2 * SPAN, x1r, PTS),
        (2, x2r, SPAN, x2r, PTS),
        (3, x1r, 2 * SPAN + 4 * S, x1r, SPAN + PTS),
    )
    for mask, ref, at, info, info_at in sources:
        first = (pos ^ mask) * 64
        for j in range(4):
            row = pl.multiple_of(first + 16 * j, 16)
            rgbt[pl.ds(row, 16), :] = ref[:, at + j * S : at + (j + 1) * S]
            lane = info_at + SKEL_LANE + j
            skel[pl.ds(row, 16), :] = jnp.broadcast_to(info[:, lane : lane + 1], (16, 128))
    e1[:F, :S] = pick(pay[:F], one_hot_rows(skel[:, :1], pos * S, S), NT)
    e1[F:32, :S] = product(pay[F:], rgbt[...], NT)
    e1[:32, S:] = jnp.zeros((32, INFO), f32)
    for b, ref in enumerate((ckeep, c8, c6, c14)):
        e1[32 + 16 * b : 48 + 16 * b] = ref[...]


CLUSTER_MASKS = (0, 8, 6, 14)


def cluster_up(e1, r1, e2, rcbt, skel):
    d = lax.axis_index("leaf")
    gk = (d >> 2) & 3
    for m, ref, at in ((0, e1, 32), (2, e1, 96), (1, r1, 32), (3, r1, 96)):
        for b, mask in enumerate(CLUSTER_MASKS):
            row = pl.multiple_of(((d & 15) ^ mask ^ m) * 16, 16)
            rows = slice(at + 16 * b, at + 16 * b + 16)
            rcbt[pl.ds(row, 16), :] = ref[rows, :S]
            skel[pl.ds(row, 16), :] = ref[rows, S:]
    group = e1[:32, :S] + r1[:32, :S]
    e2[:, :S] = group
    e2[:F, S:] = pick(group[:F], one_hot_rows(skel[:, :1], gk * S, S), NT)
    e2[F:, S:] = product(group[F:], rcbt[...], NT)


def interact(left, other_points, other_weights):
    values = jnp.exp2(dot(left, exponent_rows(other_points, False), NN))
    return product(other_weights, values, NT)


def early_field(e2, h, cpay, c1, c2, side, top):
    left = jnp.transpose(exponent_rows(e2[:F, :S], True))
    side[...] = interact(
        left,
        jnp.concatenate([e2[:F, S : 2 * S], h[:F, : 2 * S]], 1),
        jnp.concatenate([e2[F:, S : 2 * S], h[F:, : 2 * S]], 1),
    )
    left = jnp.transpose(exponent_rows(cpay[:F], True))
    top[...] = interact(
        left, jnp.concatenate([c1[:F], c2[:F]], 1), jnp.concatenate([c1[F:], c2[F:]], 1)
    )


def downward(cpay, c3, side, top, rcbt, rgbt, device, leaf, far):
    left = jnp.transpose(exponent_rows(cpay[:F], True))
    total = top[...] + interact(left, c3[:F], c3[F:])
    down_group = side[...] + product(total, rcbt[...], NN)
    down_device = product(down_group, rgbt[...], NN)
    down_leaves = product(down_device, device[...], NT)
    for l in range(LEAVES_DEV):
        far[:, l * LEAF : (l + 1) * LEAF] = product(
            down_leaves[:, l * S : (l + 1) * S], leaf[l * LEAF : (l + 1) * LEAF], NT
        )


def work_items(info):
    d = lax.axis_index("leaf")
    row = lax.broadcasted_iota(jnp.int32, info.shape, 0)
    lane = lax.broadcasted_iota(jnp.int32, info.shape, 1)
    owner = info >> 2
    step = owner - d
    even8 = (d & 8) == 0
    even4 = (d & 4) == 0
    shard = jnp.where((step == 8) == even8, 1, 2)
    shard = jnp.where(jnp.abs(step) == 4, jnp.where((step == 4) == even4, 3, 4), shard)
    shard = jnp.where(step == 0, 0, shard)
    item = ((shard * 4 + (info & 3)) << 4) | row
    mine = ((owner & 3) == (d & 3)) & (lane < info[:, NBR : NBR + 1])
    return jnp.where(lane == NBR, info, jnp.where(mine, item, -1))


def make_work(items, work, first_leaf, filled):
    def list_leaf(leaf, filled):
        def list_slots(step, filled):
            for u in range(8):
                item = items[leaf, step * 8 + u]
                work[filled] = item
                filled += 1 + (item >> 31)
            return filled

        return lax.fori_loop(0, (items[leaf, NBR] + 7) >> 3, list_slots, filled)

    return lax.fori_loop(first_leaf, first_leaf + 8, list_leaf, filled)


def run_tiles(first, last, work, left, right, charge, acc):
    def tiles(start, number):
        items = [work[start + u] for u in range(number)]
        pairs = [(item >> 4, item & 15) for item in items]
        exponents = [dot(left[source], right[target], NN) for source, target in pairs]
        sums = [
            dot(charge[source], jnp.exp2(exponent).astype(bf16), NN)
            for (source, _), exponent in zip(pairs, exponents)
        ]
        for (_, target), total in zip(pairs, sums):
            acc[target] += total

    def several(step, _):
        tiles(first + step * UNROLL, UNROLL)
        return 0

    whole = (last - first) // UNROLL
    lax.fori_loop(0, whole, several, 0)

    def single(n, _):
        tiles(n, 1)
        return 0

    lax.fori_loop(first + whole * UNROLL, last, single, 0)


PARTS = (0, 3, 6, 9, 13, 16)


def bounds(work, part):
    given = work[WORK - 2]
    count = work[WORK - 1]

    def edge(i):
        if i == len(PARTS) - 1:
            return count
        at = ((count * PARTS[i]) >> 4) & -UNROLL
        return jnp.maximum(at, given) if i == len(PARTS) - 2 else at

    return edge(part), edge(part + 1)


def source_rows(ref, shard, left, charge):
    for l in range(LEAVES_DEV):
        cols = slice(l * LEAF, (l + 1) * LEAF)
        left[4 * shard + l] = jnp.transpose(exponent_rows(ref[:F, cols], True))
        charge[4 * shard + l] = ref[F:, cols].astype(bf16)


def target_rows(ref, at, q, right):
    for l in range(LEAVES_DEV):
        right[4 * q + l] = exponent_rows(ref[:F, at + l * LEAF : at + (l + 1) * LEAF], False)


def near_plan(items, w, x2r, x1r, left, right, charge, work):
    given = make_work(items, work, 0, 0)
    count = make_work(items, work, 8, given)
    work[WORK - 2] = given
    work[WORK - 1] = count
    source_rows(w, 0, left, charge)
    for q, (ref, at) in enumerate(((x1r, 0), (x1r, SPAN), (w, 0), (x2r, 0))):
        target_rows(ref, at, q, right)


def near_start(work, w8, i8, w4, i4, right, left0, charge0, acc, left, charge):
    del left0, charge0
    for i, ref in enumerate((w8, i8, w4, i4)):
        source_rows(ref, 1 + i, left, charge)
    acc[...] = jnp.zeros_like(acc)
    run_tiles(*bounds(work, 0), work, left, right, charge, acc)


def near_more(part):
    def body(work, left, right, charge, before, acc, *give):
        del before
        run_tiles(*bounds(work, part), work, left, right, charge, acc)
        for ref in give:
            copy_out(acc, 0, ref)

    return body


def copy_out(acc, first, ref):
    for q in range(2):
        for l in range(LEAVES_DEV):
            ref[q, :, l * LEAF : (l + 1) * LEAF] = acc[first + 4 * q + l]


def near_last(work, left, right, charge, before, keep, acc):
    acc[8:] = before[8:]
    run_tiles(*bounds(work, len(PARTS) - 2), work, left, right, charge, acc)
    copy_out(acc, 8, keep)


WORK = 16 * NBR + 16


def program(
    points,
    charges,
    near_list,
    near_count,
    leaf_basis,
    device_basis,
    device_skeleton,
    group_basis,
    group_skeleton,
    cluster_basis,
    cluster_skeleton,
):
    w, x2, gnext, gkeep, ckeep, c8, c6, c14 = call(
        pack_first,
        (
            out(32, PTS),
            out(16, SPAN + 8 * S),
            out(16, 4 * S),
            out(16, 4 * S),
            out(16, BLOCK),
            out(16, BLOCK),
            out(16, BLOCK),
            out(16, BLOCK),
        ),
        (
            points,
            charges,
            near_list,
            near_count,
            group_skeleton.reshape(1, 64),
            cluster_skeleton.reshape(1, 16),
            group_basis.T,
            cluster_basis.T,
        ),
        hbm=range(8),
        scratch=(
            pltpu.VMEM((8, 128), f32),
            pltpu.VMEM((LEAVES_DEV, NBR), jnp.int32),
            pltpu.SMEM((LEAVES_DEV,), jnp.int32),
            pltpu.VMEM((1, 64), jnp.int32),
            pltpu.VMEM((1, 16), jnp.int32),
            pltpu.VMEM((64, 4 * S), f32),
            pltpu.VMEM((16, 4 * S), f32),
            pltpu.SemaphoreType.DMA((9,)),
        ),
    )
    x2r = partner(x2, 2)
    c8r = partner(c8, 8)
    c6r = partner(c6, 6)
    c14r = partner(c14, 14)
    w4r = partner(w, 4)
    w8r = partner(w, 8)
    i8r = staggered(w, 8)
    i4r = staggered(w, 4)
    x1r = partner(
        jnp.concatenate([x2[:, :SPAN], x2r[:, :SPAN], gnext, x2r[:, SPAN + 4 * S :]], 1), 1
    )
    (pay,) = call(
        device_up,
        (out(32, S),),
        (w, leaf_basis, device_basis, device_skeleton),
        hbm=(1, 2, 3),
        scratch=(
            pltpu.VMEM((PTS, S), f32),
            pltpu.VMEM((LEAVES_DEV * S, S), f32),
            pltpu.VMEM((1, S), jnp.int32),
            pltpu.SemaphoreType.DMA((LEAVES_DEV + 2,)),
        ),
    )
    e1, rgbt, _ = call(
        group_up,
        (out(96, BLOCK), out(S, S), out(S, 128)),
        (pay, x2, x2r, x1r, gkeep, ckeep, c8r, c6r, c14r),
    )
    g2 = partner(e1, 2)
    e1 = jnp.concatenate([e1[:32] + g2[:32], e1[32:], g2[32:]], 0)
    g1 = partner(e1, 1)
    e2, rcbt, _ = call(cluster_up, (out(32, 2 * S), out(S, S), out(S, 128)), (e1, g1))
    h8 = partner(e2, 8)
    e2 = jnp.concatenate([e2[:, :S], h8[:, :S], e2[:, S:] + h8[:, S:]], 1)
    h6 = partner(e2, 6)
    cpay = e2[:, 2 * S :] + h6[:, 2 * S :]
    c1 = partner(cpay, 24)
    pair = jnp.concatenate([cpay, c1], 1)
    c2 = partner(pair, 32)
    c3 = partner(jnp.concatenate([pair, c2], 1), 96)
    side, top = call(early_field, (out(16, S), out(16, S)), (e2, h6, cpay, c1, c2))

    info = jnp.concatenate(
        [x1r[:4, PTS:SPAN], x1r[:4, SPAN + PTS : 2 * SPAN], x2[:4, PTS:SPAN], x2r[:4, PTS:SPAN]],
        0,
    )
    items = work_items(info.astype(jnp.int32))
    rows = (
        jax.ShapeDtypeStruct((20, LEAF, 128), bf16),
        jax.ShapeDtypeStruct((16, 128, LEAF), bf16),
        jax.ShapeDtypeStruct((20, R, LEAF), bf16),
    )
    left, right, charge, work = call(
        near_plan,
        (*rows, jax.ShapeDtypeStruct((WORK,), jnp.int32)),
        (items, w, x2r, x1r),
        smem=(0,),
        smem_outs=(3,),
    )
    acc, left, charge = call(
        near_start,
        (out(16, R, LEAF), rows[0], rows[2]),
        (work, w8r, i8r, w4r, i4r, right, left, charge),
        smem=(0,),
        aliases={6: 1, 7: 2},
    )
    for part in range(1, len(PARTS) - 2):
        acc, *give = call(
            near_more(part),
            (out(16, R, LEAF),) + (out(2, R, PTS),) * (part == len(PARTS) - 3),
            (work, left, right, charge, acc),
            smem=(0,),
            aliases={4: 0},
        )
    got = partner(give[0], 1)
    (keep,) = call(
        near_last,
        (out(2, R, PTS),),
        (work, left, right, charge, acc),
        smem=(0,),
        scratch=(pltpu.VMEM((16, R, LEAF), f32),),
    )
    near = keep[0] + got[0] + partner(keep[1] + got[1], 2)
    (far,) = call(
        downward, (out(16, PTS),), (cpay, c3, side, top, rcbt, rgbt, device_basis, leaf_basis)
    )
    return near + far


def solution(mesh):
    return jax.shard_map(
        program,
        mesh=mesh,
        in_specs=(
            P(None, "leaf"),
            P(None, "leaf"),
            P("leaf", None),
            P("leaf"),
            P("leaf", None),
            P("leaf", None),
            P("leaf", None),
            P(None, "leaf"),
            P("leaf"),
            P(None, "leaf"),
            P("leaf"),
        ),
        out_specs=P(None, "leaf"),
        check_vma=False,
    )
```

```python
import jax
import jax.numpy as jnp
from jax import lax
from jax.experimental import pallas as pl
from jax.experimental.pallas import tpu as pltpu
from jax.sharding import PartitionSpec as P


F = 16
R = 16
LEAF = 512
S = 256
NBR = 32
LEAVES_DEV = 4
PTS = LEAVES_DEV * LEAF
INFO = 128
SKEL_LANE = 68
POINT_SCALE = 0.42466090014400953
UNROLL = 4

f32 = jnp.float32
bf16 = jnp.bfloat16

NN = (((1,), (0,)), ((), ()))
NT = (((1,), (1,)), ((), ()))


def partner(value, mask):
    size = lax.axis_size("leaf")
    return lax.ppermute(value, "leaf", [(source, source ^ mask) for source in range(size)])


def staggered(value, step):
    size = lax.axis_size("leaf")
    pairs = [
        (source, target if 0 <= target < size else source)
        for source, target in (
            (source, source + (step if source // step % 2 else -step)) for source in range(size)
        )
    ]
    return lax.ppermute(value, "leaf", pairs)


def call(body, outs, args, smem=(), hbm=(), scratch=(), smem_outs=(), aliases=None):
    spaces = [
        pltpu.SMEM if i in smem else pltpu.HBM if i in hbm else pltpu.VMEM
        for i in range(len(args))
    ]
    args = [
        pltpu.with_memory_space_constraint(arg, pltpu.HBM) if i in hbm else arg
        for i, arg in enumerate(args)
    ]
    return pl.pallas_call(
        body,
        out_shape=tuple(outs),
        in_specs=[pl.BlockSpec(memory_space=space) for space in spaces],
        out_specs=tuple(
            pl.BlockSpec(memory_space=pltpu.SMEM if i in smem_outs else pltpu.VMEM)
            for i in range(len(outs))
        ),
        input_output_aliases=aliases or {},
        scratch_shapes=list(scratch),
        compiler_params=pltpu.CompilerParams(vmem_limit_bytes=24 << 20),
    )(*args)


def out(*shape):
    return jax.ShapeDtypeStruct(shape, f32)


def split2(x):
    high = x.astype(bf16)
    return high, (x - high.astype(f32)).astype(bf16)


def split3(x):
    high = x.astype(bf16)
    rest = x - high.astype(f32)
    middle = rest.astype(bf16)
    return high, middle, (rest - middle.astype(f32)).astype(bf16)


def dot(a, b, dims):
    return lax.dot_general(a, b, dims, preferred_element_type=f32)


def product(a, b, dims):
    ah, al = split2(a)
    bh, bl = split2(b)
    rows = a.shape[0]
    both = dot(jnp.concatenate([ah, al], 0), bh, dims)
    return both[:rows] + both[rows:] + dot(ah, bl, dims)


def pick(points, one_hot, dims):
    parts = dot(jnp.concatenate(split3(points), 0), one_hot, dims)
    return parts[:F] + parts[F : 2 * F] + parts[2 * F :]


def one_hot_rows(index_column, first, width):
    lanes = lax.broadcasted_iota(jnp.int32, (index_column.shape[0], width), 1)
    return jnp.where(lanes + first == index_column.astype(jnp.int32), 1.0, 0.0).astype(bf16)


def exponent_rows(points, left):
    scaled = points * POINT_SCALE
    h, m, l = split3(scaled)
    n = points.shape[1]
    nh, nm, nl = split3(-0.5 * jnp.sum(scaled * scaled, axis=0, keepdims=True))
    row = lax.broadcasted_iota(jnp.int32, (16, n), 0)
    first = 0 if left else 3
    block = jnp.where((row >= 3 - first) & (row < 6 - first), 1.0, 0.0)
    for i, part in enumerate((nh, nm, nl)):
        block = jnp.where(row == first + i, part.astype(f32), block)
    block = block.astype(bf16)
    zero = jnp.zeros((16, n), bf16)
    if left:
        return jnp.concatenate([h, h, m, m, h, l, block, zero], 0)
    return jnp.concatenate([h, m, h, m, l, h, block, zero], 0)


SPAN = PTS + INFO
BLOCK = S + INFO


def skeleton_column(row_ref, count, tile):
    tile[...] = jnp.zeros((8, 128), f32)
    tile[0:1, :count] = row_ref[:, :count].astype(f32)
    return jnp.transpose(tile[...])


def pack_first(
    points, charges, near_list, near_count, gskel, cskel, gbt, cbt,
    w, x2, gnext, gkeep, ckeep, c8, c6, c14,
    tile, lists, counts, grow, crow, group, cluster, sems,
):
    d = lax.axis_index("leaf")
    pos = d & 3
    gk = (d >> 2) & 3
    small = [
        pltpu.make_async_copy(source, target, sems.at[i])
        for i, (source, target) in enumerate(
            (
                (near_list, lists),
                (near_count, counts),
                (gskel, grow),
                (cskel, crow),
                (gbt, group),
                (cbt, cluster),
            )
        )
    ]
    cols = pl.ds(0, PTS)
    large = [
        pltpu.make_async_copy(source, target, sems.at[6 + i])
        for i, (source, target) in enumerate(
            (
                (points, w.at[pl.ds(0, F)]),
                (charges, w.at[pl.ds(F, R)]),
                (points, x2.at[:, cols]),
            )
        )
    ]
    for copy in small + large:
        copy.start()
    x2[:, PTS:SPAN] = jnp.zeros((F, INFO), f32)
    for copy in small:
        copy.wait()
    x2[:4, PTS : PTS + NBR] = lists[...].astype(f32)
    for l in range(LEAVES_DEV):
        x2[l : l + 1, PTS + NBR : PTS + NBR + 1] = jnp.full((1, 1), counts[l], jnp.int32).astype(f32)
    column = skeleton_column(grow, 64, tile)
    for j in range(4):
        lane = PTS + SKEL_LANE + j
        x2[:, lane : lane + 1] = column[16 * j : 16 * j + 16, :1]
    for ref, start, mask in ((x2, SPAN, 2), (x2, SPAN + 4 * S, 3), (gkeep, 0, 0), (gnext, 0, 1)):
        lane = pl.multiple_of((pos ^ mask) * S, S)
        for j in range(4):
            at = start + j * S
            ref[:, at : at + S] = group[16 * j : 16 * j + 16, pl.ds(lane, S)]
    column = jnp.broadcast_to(skeleton_column(crow, 16, tile)[:16, :1], (16, INFO))
    for ref, mask in ((ckeep, 0), (c8, 2), (c6, 1), (c14, 3)):
        ref[:, :S] = cluster[:, pl.ds(pl.multiple_of((gk ^ mask) * S, S), S)]
        ref[:, S:] = column
    for copy in large:
        copy.wait()


def device_up(w, leaf_hbm, device_hbm, skeleton_hbm, pay, leaf, device, skeleton, sems):
    copies = []
    for l in range(LEAVES_DEV):
        rows = pl.ds(l * LEAF, LEAF)
        copies.append(pltpu.make_async_copy(leaf_hbm.at[rows], leaf.at[rows], sems.at[l]))
    last = pltpu.make_async_copy(device_hbm, device, sems.at[LEAVES_DEV])
    index = pltpu.make_async_copy(skeleton_hbm, skeleton, sems.at[LEAVES_DEV + 1])
    index.start()
    for copy in copies:
        copy.start()
    last.start()
    index.wait()
    rows = lax.broadcasted_iota(jnp.int32, (PTS, S), 0)
    one_hot = jnp.where(rows == skeleton[...], 1.0, 0.0).astype(bf16)
    pay[:F] = pick(w[:F], one_hot, NN)
    weights = []
    for l in range(LEAVES_DEV):
        copies[l].wait()
        weights.append(
            product(w[F:, l * LEAF : (l + 1) * LEAF], leaf[l * LEAF : (l + 1) * LEAF], NN)
        )
    last.wait()
    pay[F:] = product(jnp.concatenate(weights, 1), device[...], NN)


def group_up(pay, x2, x2r, x1r, gkeep, ckeep, c8, c6, c14, e1, rgbt, skel):
    pos = lax.axis_index("leaf") & 3
    sources = (
        (0, gkeep, 0, x2, PTS),
        (1, x1r, 2 * SPAN, x1r, PTS),
        (2, x2r, SPAN, x2r, PTS),
        (3, x1r, 2 * SPAN + 4 * S, x1r, SPAN + PTS),
    )
    for mask, ref, at, info, info_at in sources:
        first = (pos ^ mask) * 64
        for j in range(4):
            row = pl.multiple_of(first + 16 * j, 16)
            rgbt[pl.ds(row, 16), :] = ref[:, at + j * S : at + (j + 1) * S]
            lane = info_at + SKEL_LANE + j
            skel[pl.ds(row, 16), :] = jnp.broadcast_to(info[:, lane : lane + 1], (16, 128))
    e1[:F, :S] = pick(pay[:F], one_hot_rows(skel[:, :1], pos * S, S), NT)
    e1[F:32, :S] = product(pay[F:], rgbt[...], NT)
    e1[:32, S:] = jnp.zeros((32, INFO), f32)
    for b, ref in enumerate((ckeep, c8, c6, c14)):
        e1[32 + 16 * b : 48 + 16 * b] = ref[...]


CLUSTER_MASKS = (0, 8, 6, 14)


def cluster_up(e1, r1, e2, rcbt, skel):
    d = lax.axis_index("leaf")
    gk = (d >> 2) & 3
    for m, ref, at in ((0, e1, 32), (2, e1, 96), (1, r1, 32), (3, r1, 96)):
        for b, mask in enumerate(CLUSTER_MASKS):
            row = pl.multiple_of(((d & 15) ^ mask ^ m) * 16, 16)
            rows = slice(at + 16 * b, at + 16 * b + 16)
            rcbt[pl.ds(row, 16), :] = ref[rows, :S]
            skel[pl.ds(row, 16), :] = ref[rows, S:]
    group = e1[:32, :S] + r1[:32, :S]
    e2[:, :S] = group
    e2[:F, S:] = pick(group[:F], one_hot_rows(skel[:, :1], gk * S, S), NT)
    e2[F:, S:] = product(group[F:], rcbt[...], NT)


def interact(left, other_points, other_weights):
    values = jnp.exp2(dot(left, exponent_rows(other_points, False), NN))
    return product(other_weights, values, NT)


def early_field(e2, h, cpay, c1, c2, side, top):
    left = jnp.transpose(exponent_rows(e2[:F, :S], True))
    side[...] = interact(
        left,
        jnp.concatenate([e2[:F, S : 2 * S], h[:F, : 2 * S]], 1),
        jnp.concatenate([e2[F:, S : 2 * S], h[F:, : 2 * S]], 1),
    )
    left = jnp.transpose(exponent_rows(cpay[:F], True))
    top[...] = interact(
        left, jnp.concatenate([c1[:F], c2[:F]], 1), jnp.concatenate([c1[F:], c2[F:]], 1)
    )


def downward(cpay, c3, side, top, rcbt, rgbt, device, leaf, keep, got, rest, far):
    left = jnp.transpose(exponent_rows(cpay[:F], True))
    total = top[...] + interact(left, c3[:F], c3[F:])
    down_group = side[...] + product(total, rcbt[...], NN)
    down_device = product(down_group, rgbt[...], NN)
    down_leaves = product(down_device, device[...], NT)
    for l in range(LEAVES_DEV):
        cols = slice(l * LEAF, (l + 1) * LEAF)
        near = keep[0, :, cols] + got[0, :, cols] + rest[:, cols]
        far[:, cols] = near + product(down_leaves[:, l * S : (l + 1) * S], leaf[cols], NT)


def work_items(info):
    d = lax.axis_index("leaf")
    row = lax.broadcasted_iota(jnp.int32, info.shape, 0)
    lane = lax.broadcasted_iota(jnp.int32, info.shape, 1)
    owner = info >> 2
    step = owner - d
    even8 = (d & 8) == 0
    even4 = (d & 4) == 0
    shard = jnp.where((step == 8) == even8, 1, 2)
    shard = jnp.where(jnp.abs(step) == 4, jnp.where((step == 4) == even4, 3, 4), shard)
    shard = jnp.where(step == 0, 0, shard)
    item = ((shard * 4 + (info & 3)) << 4) | row
    mine = ((owner & 3) == (d & 3)) & (lane < info[:, NBR : NBR + 1])
    return jnp.where(lane == NBR, info, jnp.where(mine, item, -1))


def make_work(items, work, first_leaf, filled):
    def list_leaf(leaf, filled):
        def list_slots(step, filled):
            for u in range(8):
                item = items[leaf, step * 8 + u]
                work[filled] = item
                filled += 1 + (item >> 31)
            return filled

        return lax.fori_loop(0, (items[leaf, NBR] + 7) >> 3, list_slots, filled)

    return lax.fori_loop(first_leaf, first_leaf + 8, list_leaf, filled)


def run_tiles(first, last, work, left, right, charge, acc):
    def tiles(start, number):
        items = [work[start + u] for u in range(number)]
        pairs = [(item >> 4, item & 15) for item in items]
        exponents = [dot(left[source], right[target], NN) for source, target in pairs]
        sums = [
            dot(charge[source], jnp.exp2(exponent).astype(bf16), NN)
            for (source, _), exponent in zip(pairs, exponents)
        ]
        for (_, target), total in zip(pairs, sums):
            acc[target] += total

    def several(step, _):
        tiles(first + step * UNROLL, UNROLL)
        return 0

    whole = (last - first) // UNROLL
    lax.fori_loop(0, whole, several, 0)

    def single(n, _):
        tiles(n, 1)
        return 0

    lax.fori_loop(first + whole * UNROLL, last, single, 0)


PARTS = (0, 3, 6, 9, 13, 16)


def bounds(work, part):
    given = work[WORK - 2]
    count = work[WORK - 1]

    def edge(i):
        if i == len(PARTS) - 1:
            return count
        at = ((count * PARTS[i]) >> 4) & -UNROLL
        return jnp.maximum(at, given) if i == len(PARTS) - 2 else at

    return edge(part), edge(part + 1)


def source_rows(ref, shard, left, charge):
    for l in range(LEAVES_DEV):
        cols = slice(l * LEAF, (l + 1) * LEAF)
        left[4 * shard + l] = jnp.transpose(exponent_rows(ref[:F, cols], True))
        charge[4 * shard + l] = ref[F:, cols].astype(bf16)


def target_rows(ref, at, q, right):
    for l in range(LEAVES_DEV):
        right[4 * q + l] = exponent_rows(ref[:F, at + l * LEAF : at + (l + 1) * LEAF], False)


def near_plan(items, w, x2r, x1r, left, right, charge, work):
    given = make_work(items, work, 0, 0)
    count = make_work(items, work, 8, given)
    work[WORK - 2] = given
    work[WORK - 1] = count
    source_rows(w, 0, left, charge)
    for q, (ref, at) in enumerate(((x1r, 0), (x1r, SPAN), (w, 0), (x2r, 0))):
        target_rows(ref, at, q, right)


def near_start(work, w8, i8, w4, i4, right, left0, charge0, acc, left, charge):
    del left0, charge0
    for i, ref in enumerate((w8, i8, w4, i4)):
        source_rows(ref, 1 + i, left, charge)
    acc[...] = jnp.zeros_like(acc)
    run_tiles(*bounds(work, 0), work, left, right, charge, acc)


def near_more(part):
    def body(work, left, right, charge, before, acc, *give):
        del before
        run_tiles(*bounds(work, part), work, left, right, charge, acc)
        for ref in give:
            copy_out(acc, 0, ref)

    return body


def copy_out(acc, first, ref):
    for q in range(2):
        for l in range(LEAVES_DEV):
            ref[q, :, l * LEAF : (l + 1) * LEAF] = acc[first + 4 * q + l]


def near_last(work, left, right, charge, before, keep, acc):
    acc[8:] = before[8:]
    run_tiles(*bounds(work, len(PARTS) - 2), work, left, right, charge, acc)
    copy_out(acc, 8, keep)


WORK = 16 * NBR + 16


def program(
    points,
    charges,
    near_list,
    near_count,
    leaf_basis,
    device_basis,
    device_skeleton,
    group_basis,
    group_skeleton,
    cluster_basis,
    cluster_skeleton,
):
    w, x2, gnext, gkeep, ckeep, c8, c6, c14 = call(
        pack_first,
        (
            out(32, PTS),
            out(16, SPAN + 8 * S),
            out(16, 4 * S),
            out(16, 4 * S),
            out(16, BLOCK),
            out(16, BLOCK),
            out(16, BLOCK),
            out(16, BLOCK),
        ),
        (
            points,
            charges,
            near_list,
            near_count,
            group_skeleton.reshape(1, 64),
            cluster_skeleton.reshape(1, 16),
            group_basis.T,
            cluster_basis.T,
        ),
        hbm=range(8),
        scratch=(
            pltpu.VMEM((8, 128), f32),
            pltpu.VMEM((LEAVES_DEV, NBR), jnp.int32),
            pltpu.SMEM((LEAVES_DEV,), jnp.int32),
            pltpu.VMEM((1, 64), jnp.int32),
            pltpu.VMEM((1, 16), jnp.int32),
            pltpu.VMEM((64, 4 * S), f32),
            pltpu.VMEM((16, 4 * S), f32),
            pltpu.SemaphoreType.DMA((9,)),
        ),
    )
    x2r = partner(x2, 2)
    c8r = partner(c8, 8)
    c6r = partner(c6, 6)
    c14r = partner(c14, 14)
    w4r = partner(w, 4)
    w8r = partner(w, 8)
    i8r = staggered(w, 8)
    i4r = staggered(w, 4)
    x1r = partner(
        jnp.concatenate([x2[:, :SPAN], x2r[:, :SPAN], gnext, x2r[:, SPAN + 4 * S :]], 1), 1
    )
    (pay,) = call(
        device_up,
        (out(32, S),),
        (w, leaf_basis, device_basis, device_skeleton),
        hbm=(1, 2, 3),
        scratch=(
            pltpu.VMEM((PTS, S), f32),
            pltpu.VMEM((LEAVES_DEV * S, S), f32),
            pltpu.VMEM((1, S), jnp.int32),
            pltpu.SemaphoreType.DMA((LEAVES_DEV + 2,)),
        ),
    )
    e1, rgbt, _ = call(
        group_up,
        (out(96, BLOCK), out(S, S), out(S, 128)),
        (pay, x2, x2r, x1r, gkeep, ckeep, c8r, c6r, c14r),
    )
    g2 = partner(e1, 2)
    e1 = jnp.concatenate([e1[:32] + g2[:32], e1[32:], g2[32:]], 0)
    g1 = partner(e1, 1)
    e2, rcbt, _ = call(cluster_up, (out(32, 2 * S), out(S, S), out(S, 128)), (e1, g1))
    h8 = partner(e2, 8)
    e2 = jnp.concatenate([e2[:, :S], h8[:, :S], e2[:, S:] + h8[:, S:]], 1)
    h6 = partner(e2, 6)
    cpay = e2[:, 2 * S :] + h6[:, 2 * S :]
    c1 = partner(cpay, 24)
    pair = jnp.concatenate([cpay, c1], 1)
    c2 = partner(pair, 32)
    c3 = partner(jnp.concatenate([pair, c2], 1), 96)
    side, top = call(early_field, (out(16, S), out(16, S)), (e2, h6, cpay, c1, c2))

    info = jnp.concatenate(
        [x1r[:4, PTS:SPAN], x1r[:4, SPAN + PTS : 2 * SPAN], x2[:4, PTS:SPAN], x2r[:4, PTS:SPAN]],
        0,
    )
    items = work_items(info.astype(jnp.int32))
    rows = (
        jax.ShapeDtypeStruct((20, LEAF, 128), bf16),
        jax.ShapeDtypeStruct((16, 128, LEAF), bf16),
        jax.ShapeDtypeStruct((20, R, LEAF), bf16),
    )
    left, right, charge, work = call(
        near_plan,
        (*rows, jax.ShapeDtypeStruct((WORK,), jnp.int32)),
        (items, w, x2r, x1r),
        smem=(0,),
        smem_outs=(3,),
    )
    acc, left, charge = call(
        near_start,
        (out(16, R, LEAF), rows[0], rows[2]),
        (work, w8r, i8r, w4r, i4r, right, left, charge),
        smem=(0,),
        aliases={6: 1, 7: 2},
    )
    for part in range(1, len(PARTS) - 2):
        acc, *give = call(
            near_more(part),
            (out(16, R, LEAF),) + (out(2, R, PTS),) * (part == len(PARTS) - 3),
            (work, left, right, charge, acc),
            smem=(0,),
            aliases={4: 0},
        )
    got = partner(give[0], 1)
    (keep,) = call(
        near_last,
        (out(2, R, PTS),),
        (work, left, right, charge, acc),
        smem=(0,),
        scratch=(pltpu.VMEM((16, R, LEAF), f32),),
    )
    rest = partner(keep[1] + got[1], 2)
    (total,) = call(
        downward,
        (out(16, PTS),),
        (cpay, c3, side, top, rcbt, rgbt, device_basis, leaf_basis, keep, got, rest),
    )
    return total


def solution(mesh):
    return jax.shard_map(
        program,
        mesh=mesh,
        in_specs=(
            P(None, "leaf"),
            P(None, "leaf"),
            P("leaf", None),
            P("leaf"),
            P("leaf", None),
            P("leaf", None),
            P("leaf", None),
            P(None, "leaf"),
            P("leaf"),
            P(None, "leaf"),
            P("leaf"),
        ),
        out_specs=P(None, "leaf"),
        check_vma=False,
    )
```
